32 devices in a mesh: seq: 16 (over z, y, core), head: 2 (over x).
Axes of the slice: x: 2, y: 2, z: 4, core: 2. Of those that a mesh axis runs over, the one named last changes fastest.
Arguments:
- latent_queries: bfloat16 [2048, 128, 576], P('seq', 'head'), may hold values from -16 to 16
- latent_keys: bfloat16 [1024, 576], P('seq'), may hold values from -6 to 6
- index_queries: bfloat16 [2048, 64, 128], P('seq', 'head'), may hold values from -8 to 8
- index_keys: bfloat16 [1024, 128], P('seq'), may hold values from -6 to 6
- head_weights: float32 [2048, 64], P('seq', 'head'), may hold values from -18 to 18
- visible: int32 [2048], P('seq'), may hold values from 1 to 1024, as said below
Outputs:
- grad_index_queries: bfloat16 [2048, 64, 128], P('seq', 'head')
- grad_head_weights: float32 [2048, 64], P('seq', 'head')
- grad_index_keys: float32 [1024, 128], P('seq')
The draws below stay inside these ranges and needn't reach their ends.
Inputs may be any that keep to these rules, and one draw needn't show every extreme that they name: Row t sees keys 0 to visible[t] - 1, never more than (t * 1024) // 2048 + 1 of them; the last row sees all 1024 keys.
All inputs are finite; a program needn't handle non-finite values.
Results may differ from the reference program's by a relative error of at most 0.0049.
Values may be sent and summed in bfloat16 or wider, within the bound.
A program may use at most 128 MiB of HBM per device.

```python
import math
import jax
import jax.numpy as jnp
from jax import lax

LATENT = 576
MLA_HEADS = 128
INDEX_HEADS = 64
INDEX_DIM = 128
QUERIES = 2048
KEYS = 1024


def visible_counts(key):
    positions = jnp.arange(QUERIES, dtype=jnp.int32)
    baseline = positions * KEYS // QUERIES + 1
    jitter = jax.random.randint(jax.random.fold_in(key, 11), (QUERIES,), 0, KEYS // 8 + 1)
    jitter = jnp.where(positions == QUERIES - 1, 0, jitter)
    lowest = jnp.minimum(baseline, 2)
    return jnp.maximum(baseline - jitter, lowest).astype(jnp.int32)


def make_keys(key, salt, width):
    subkey = jax.random.fold_in(key, salt)
    return jnp.clip(jax.random.normal(subkey, (KEYS, width), jnp.float32), -6.0, 6.0)


def draw_visible(key, part):
    return visible_counts(key)


def draw_latent_keys(key, part):
    return make_keys(key, 1, LATENT).astype(jnp.bfloat16)


def draw_index_keys(key, part):
    return make_keys(key, 2, INDEX_DIM).astype(jnp.bfloat16)


def draw_latent_queries(key, part):
    full_shape = (QUERIES, MLA_HEADS, LATENT)
    subkey = jax.random.fold_in(key, 3)
    values = jnp.clip(jax.random.normal(subkey, full_shape, jnp.float32), -6.0, 6.0) * 2.3
    return values.astype(jnp.bfloat16)


def draw_index_queries(key, part):
    full_shape = (QUERIES, INDEX_HEADS, INDEX_DIM)
    subkey = jax.random.fold_in(key, 5)
    values = jnp.clip(jax.random.normal(subkey, full_shape, jnp.float32), -6.0, 6.0)
    return values.astype(jnp.bfloat16)


def draw_head_weights(key, part):
    subkey = jax.random.fold_in(key, 6)
    values = jnp.clip(jax.random.normal(subkey, (QUERIES, INDEX_HEADS), jnp.float32), -6.0, 6.0) * 3.0
    return values.astype(jnp.float32)


def setup_inputs(seed: int = 0) -> dict:
    streams_of = jax.random.split(jax.random.key(seed), 7)
    return {
        "latent_queries": draw_latent_queries(jax.random.fold_in(streams_of[6], 71), 0),
        "latent_keys": draw_latent_keys(jax.random.fold_in(streams_of[6], 71), 0),
        "index_queries": draw_index_queries(jax.random.fold_in(streams_of[6], 71), 0),
        "index_keys": draw_index_keys(jax.random.fold_in(streams_of[6], 71), 0),
        "head_weights": draw_head_weights(jax.random.fold_in(streams_of[6], 71), 0),
        "visible": draw_visible(jax.random.fold_in(streams_of[6], 71), 0),
    }


mla_scale = 192.0 ** -0.5
loss_weight = 16.0
neg_fill = -1.0e30


def reference(latent_queries, latent_keys, index_queries, index_keys, head_weights, visible):
    query_count = latent_queries.shape[0]
    key_count = latent_keys.shape[0]
    row_block = math.gcd(query_count, 128)
    block_count = query_count // row_block
    latent_wide = latent_keys.astype(jnp.float32)
    index_wide = index_keys.astype(jnp.float32)
    dot_scale = INDEX_DIM ** -0.5
    head_scale = INDEX_HEADS ** -0.5
    columns = jnp.arange(key_count, dtype=jnp.int32)

    def one_block(key_grad, inputs):
        lat_rows, idx_rows, weight_rows, seen_rows = inputs
        seen = columns[None, :] < seen_rows[:, None]
        scores = jnp.einsum("thl,kl->thk", lat_rows.astype(jnp.float32), latent_wide, precision=lax.Precision.HIGHEST) * mla_scale
        scores = jnp.where(seen[:, None, :], scores, neg_fill)
        maxima = jnp.max(scores, axis=2, keepdims=True)
        mla_norm = maxima + jnp.log(jnp.sum(jnp.exp(scores - maxima), axis=2, keepdims=True))
        target = jnp.sum(jnp.exp(scores - mla_norm), axis=1) / MLA_HEADS
        products = jnp.einsum("thd,kd->thk", idx_rows.astype(jnp.float32), index_wide, precision=lax.Precision.HIGHEST) * dot_scale
        active = jnp.maximum(products, 0.0)
        logits = jnp.sum(weight_rows[:, :, None] * active, axis=1) * head_scale
        logits = jnp.where(seen, logits, neg_fill)
        row_peak = jnp.max(logits, axis=1, keepdims=True)
        weights = jnp.exp(logits - row_peak)
        index_prob = weights / jnp.sum(weights, axis=1, keepdims=True)
        slope = loss_weight * (index_prob - target)
        edge_grad = jnp.where(products > 0.0, slope[:, None, :] * (weight_rows * head_scale)[:, :, None], 0.0).astype(jnp.bfloat16)
        edge_wide = edge_grad.astype(jnp.float32)
        query_grad = (jnp.einsum("thk,kd->thd", edge_wide, index_wide, precision=lax.Precision.HIGHEST) * dot_scale).astype(jnp.bfloat16)
        weight_grad = jnp.sum(slope[:, None, :] * active, axis=2) * head_scale
        key_term = jnp.einsum("thk,thd->kd", edge_wide, idx_rows.astype(jnp.float32), precision=lax.Precision.HIGHEST) * dot_scale
        return key_grad + key_term, (query_grad, weight_grad)

    inputs = (
        latent_queries.reshape(block_count, row_block, MLA_HEADS, LATENT),
        index_queries.reshape(block_count, row_block, INDEX_HEADS, INDEX_DIM),
        head_weights.reshape(block_count, row_block, INDEX_HEADS),
        visible.reshape(block_count, row_block),
    )
    key_grad, stacked = lax.scan(one_block, jnp.zeros((key_count, INDEX_DIM), jnp.float32), inputs)
    grad_index_queries = stacked[0].reshape(query_count, INDEX_HEADS, INDEX_DIM)
    grad_head_weights = stacked[1].reshape(query_count, INDEX_HEADS)
    return (grad_index_queries, grad_head_weights, key_grad)
```

```python
import functools
import jax
import jax.numpy as jnp
from jax import lax
from jax.experimental import pallas as pl
from jax.experimental.pallas import tpu as pltpu
from jax.sharding import PartitionSpec as P

MLA_HEADS = 128
INDEX_HEADS = 64
LOG2E = 1.4426950408889634

mla_scale = 192.0 ** (-0.5)
loss_weight = 16.0
neg_fill = -1e30
MESH = pl.DeviceIdType.MESH
VMEM = pltpu.VMEM
BF16 = jnp.bfloat16
F32 = jnp.float32
LANES = 256
CHUNK = 256
QUAD = 4


def line_sizes(n):
    ny = 2 if n <= 16 else 4
    return n // (2 * ny), ny


def remote(src, dst, ssem, rsem, device):
    return pltpu.make_async_remote_copy(
        src_ref=src, dst_ref=dst, send_sem=ssem, recv_sem=rsem, device_id=device, device_id_type=MESH
    )


class Gather:
    def __init__(self, n, ref, everything, lsem, zs, zr, ys, yr, cs, cr):
        self.nz, self.ny = line_sizes(n)
        self.me = lax.axis_index("seq")
        self.core = self.me % 2
        self.y = (self.me // 2) % self.ny
        self.z = self.me // (2 * self.ny)
        self.ref, self.everything = ref, everything
        self.size = ref.shape[0]
        self.lsem, self.zs, self.zr, self.ys, self.yr, self.cs, self.cr = lsem, zs, zr, ys, yr, cs, cr
        self.pending = []

    def at(self, zz, yy, cc):
        return (zz * self.ny + yy) * 2 + cc

    def rows(self, owner):
        return self.everything.at[pl.ds(pl.multiple_of(owner * self.size, self.size), self.size), :]

    def send(self, owner, device, ssem, rsem, first=False):
        src = self.ref if first else self.rows(owner)
        copy = remote(src, self.rows(owner), ssem, rsem, {"seq": device})
        copy.start()
        self.pending.append(copy)

    def receive(self, owner, ssem, rsem):
        remote(self.ref, self.rows(owner), ssem, rsem, {"seq": self.at(self.z, self.y, 1 - self.core)}).wait_recv()

    def keep(self):
        self.local = pltpu.make_async_copy(self.ref, self.rows(self.me), self.lsem)
        self.local.start()

    def start(self):
        z, y, core, nz, ny = self.z, self.y, self.core, self.nz, self.ny
        for k in range(1, nz):
            self.send(self.me, self.at((z + k) % nz, y, core), self.zs.at[k], self.zr.at[k], True)
        for j in range(1, ny):
            self.send(self.me, self.at(z, (y + j) % ny, core), self.ys.at[0, j], self.yr.at[0, j], True)
        self.send(self.me, self.at(z, y, 1 - core), self.cs.at[0, 0], self.cr.at[0, 0], True)

    def pass_z(self, k):
        z, y, core, nz, ny = self.z, self.y, self.core, self.nz, self.ny
        owner = self.at((z - k + nz) % nz, y, core)
        self.receive(owner, self.zs.at[k], self.zr.at[k])
        for j in range(1, ny):
            self.send(owner, self.at(z, (y + j) % ny, core), self.ys.at[k, j], self.yr.at[k, j])
        self.send(owner, self.at(z, y, 1 - core), self.cs.at[k, 0], self.cr.at[k, 0])

    def pass_y(self, k):
        z, y, core, nz, ny = self.z, self.y, self.core, self.nz, self.ny
        for j in range(1, ny):
            owner = self.at((z - k + nz) % nz, (y - j + ny) % ny, core)
            self.receive(owner, self.ys.at[k, j], self.yr.at[k, j])
            self.send(owner, self.at(z, y, 1 - core), self.cs.at[k, j], self.cr.at[k, j])

    def finish(self):
        z, y, core, nz, ny = self.z, self.y, self.core, self.nz, self.ny
        for k in range(nz):
            for j in range(ny):
                owner = self.at((z - k + nz) % nz, (y - j + ny) % ny, 1 - core)
                self.receive(owner, self.cs.at[k, j], self.cr.at[k, j])
        self.local.wait()

    def drain(self):
        for copy in self.pending:
            copy.wait_send()


def kernel(
    n, nh, lat_ref, idx_ref, w_ref, vis_ref, latq_hbm, iq_hbm,
    qgrad_ref, wgrad_ref, kgrad_ref,
    latq, iqraw, wide, iqt, wiq, lat_all, idx_all, ikt, kaug, eye, total, sbuf, ebuf, signs,
    logit, logit_got, part_out, part_got, slope, fold, kg_all, kg_out, got, mine, peer,
    qsem, isem, glsem, zs0, zr0, ys0, yr0, cs0, cr0, zs1, zr1, ys1, yr1, cs1, cr1,
    lgs, lgr, ps, pr, ks, kr, hs, hr,
):
    me = lax.axis_index("seq")
    head = lax.axis_index("head")
    heads, width, row_count = latq.shape
    key_count = lat_all.shape[0]
    depth = idx_ref.shape[1]
    gheads = w_ref.shape[0]
    size = idx_ref.shape[0]
    half = row_count // 2
    dot_scale = float(depth) ** (-0.5)
    head_scale = INDEX_HEADS ** (-0.5)
    nz, ny = line_sizes(n)

    barrier = pltpu.get_barrier_semaphore()
    for k in range(1, n):
        pl.semaphore_signal(barrier, inc=1, device_id={"seq": (me + k) % n}, device_id_type=MESH)
    for k in range(1, nh):
        pl.semaphore_signal(barrier, inc=1, device_id={"head": (head + k) % nh}, device_id_type=MESH)
    load_iq = pltpu.make_async_copy(iq_hbm, iqraw, isem)
    load_iq.start()
    parts = qsem.shape[0]
    per = heads // parts
    loads = [
        pltpu.make_async_copy(latq_hbm.at[pl.ds(i * per, per)], latq.at[pl.ds(i * per, per)], qsem.at[i])
        for i in range(parts)
    ]
    for c in loads:
        c.start()
    gi = Gather(n, idx_ref, idx_all, glsem.at[0], zs0, zr0, ys0, yr0, cs0, cr0)
    gl = Gather(n, lat_ref, lat_all, glsem.at[1], zs1, zr1, ys1, yr1, cs1, cr1)
    gi.keep()
    gl.keep()
    pl.semaphore_wait(barrier, n - 1 + nh - 1)
    gi.start()
    gl.start()

    load_iq.wait()
    wide[...] = iqraw[...].astype(F32)
    wcol = (w_ref[...] * head_scale).T

    for g in range(gheads):
        a = wide[pl.ds(g, row_count, stride=gheads), :]
        iqt[g // QUAD, :, (g % QUAD) * row_count : (g % QUAD + 1) * row_count] = a.T.astype(BF16)
        wiq[pl.ds(g * row_count, row_count), :] = (a * wcol[:, g : g + 1]).astype(BF16)
    first = lax.broadcasted_iota(jnp.int32, (half, LANES), 0)
    second = lax.broadcasted_iota(jnp.int32, (half, LANES), 1)
    eye[...] = jnp.where(first == second % half, 1.0, 0.0).astype(BF16)

    for k in range(1, nz):
        gi.pass_z(k)
    for k in range(nz):
        gi.pass_y(k)
    gi.finish()
    ikt[...] = idx_all[...].astype(F32).T.astype(BF16)
    logit[...] = jnp.zeros_like(logit)

    chunks = [slice(m, m + CHUNK) for m in range(0, key_count, CHUNK)]
    quads = gheads // QUAD

    def index_quad(q, _):
        w = w_ref[pl.ds(pl.multiple_of(q * QUAD, QUAD), QUAD), :] * (head_scale * dot_scale)
        queries = iqt[q]
        for m in chunks:
            p = jnp.dot(idx_all[m, :], queries, preferred_element_type=F32)
            signs[q, m, :] = p.astype(BF16)
            added = None
            for j in range(QUAD):
                x = jnp.maximum(p[:, j * row_count : (j + 1) * row_count], 0.0) * w[j : j + 1]
                added = x if added is None else added + x
            logit[m, :] += added
        return 0

    done = 0
    for k in range(1, nz):
        upto = quads * k // nz
        lax.fori_loop(done, upto, index_quad, 0)
        done = upto
        gl.pass_z(k)
    lax.fori_loop(done, quads, index_quad, 0)
    head_peers = [(head + k) % nh for k in range(1, nh)]
    sent = []
    for k, to in enumerate(head_peers):
        sent.append(remote(logit, logit_got.at[k], lgs.at[k], lgr.at[k], {"head": to}))
        sent[-1].start()
    for k in range(nz):
        gl.pass_y(k)
    gl.finish()
    for c in loads:
        c.wait()

    c2 = mla_scale * LOG2E
    group = LANES // half
    groups = heads // group
    kaug[:, :width] = lat_all[...]
    lane = lax.broadcasted_iota(jnp.int32, (key_count // 2, row_count), 1)
    for r in range(2):
        r0 = r * half
        ids = lax.broadcasted_iota(jnp.int32, (key_count, half), 0)
        kaug[:, width:] = jnp.where(ids < vis_ref[:, r0 : r0 + half], 0.0, neg_fill).astype(BF16)
        total[...] = jnp.zeros_like(total)

        def step(g, slot, peak, inv, r0=r0):
            if g is not None:
                several = [latq[g * group + i][:, r0 : r0 + half] for i in range(group)]
                queries = jnp.concatenate([jnp.concatenate(several, axis=1), eye[...]], axis=0)
            high = low = None
            for m in chunks:
                if inv is not None:
                    t = ebuf[slot, m, :] * inv
                    total[m, :] += t[:, : LANES // 2] + t[:, LANES // 2 :]
                if g is not None:
                    s = jnp.dot(kaug[m, :], queries, preferred_element_type=F32)
                    sbuf[slot, m, :] = s
                    t = jnp.max(s.reshape(-1, 8, LANES), axis=0)
                    high = t if high is None else jnp.maximum(high, t)
                if peak is not None:
                    e = jnp.exp2((sbuf[1 - slot, m, :] - peak) * c2)
                    ebuf[1 - slot, m, :] = e
                    t = jnp.sum(e.reshape(-1, 8, LANES), axis=0)
                    low = t if low is None else low + t
            next_peak = None if g is None else jnp.max(high, axis=0, keepdims=True)
            next_inv = None if peak is None else (1.0 / MLA_HEADS) / jnp.sum(low, axis=0, keepdims=True)
            return next_peak, next_inv

        peak, _ = step(0, 0, None, None)
        peak, inv = step(1, 1, peak, None)

        def two(i, carry):
            carry = step(2 * i + 2, 0, *carry)
            return step(2 * i + 3, 1, *carry)

        peak, inv = lax.fori_loop(0, groups // 2 - 1, two, (peak, inv))
        _, inv = step(None, 0, peak, inv)
        step(None, 1, None, inv)

        t = total[...]
        t = t + pltpu.roll(t, half, 1)
        folded = jnp.where(lane < half, t[: key_count // 2], t[key_count // 2 :])
        fold[r] = folded
        part_out[r] = folded.astype(BF16)
        for k, to in enumerate(head_peers):
            sent.append(remote(part_out.at[r], part_got.at[k, r], ps.at[k, r], pr.at[k, r], {"head": to}))
            sent[-1].start()

    for k in range(nh - 1):
        remote(logit, logit_got.at[k], lgs.at[k], lgr.at[k], {"head": head_peers[k]}).wait_recv()
    both = logit[...]
    for k in range(nh - 1):
        both = both + logit_got[k]
    ids = lax.broadcasted_iota(jnp.int32, (key_count, row_count), 0)
    both = jnp.where(ids < vis_ref[...], both, neg_fill)
    weights = jnp.exp(both - jnp.max(both, axis=0, keepdims=True))
    total[...] = weights * (1.0 / jnp.sum(weights, axis=0, keepdims=True))
    folds = []
    for r in range(2):
        t = fold[r]
        for k in range(nh - 1):
            remote(part_out.at[r], part_got.at[k, r], ps.at[k, r], pr.at[k, r], {"head": head_peers[k]}).wait_recv()
            t = t + part_got[k, r].astype(F32)
        folds.append(t)
    upper = jnp.where(lane < half, folds[0], pltpu.roll(folds[1], half, 1))
    lower = jnp.where(lane < half, pltpu.roll(folds[0], half, 1), folds[1])
    slope[: key_count // 2, :] = (loss_weight * (total[: key_count // 2, :] - upper)).astype(BF16)
    slope[key_count // 2 :, :] = (loss_weight * (total[key_count // 2 :, :] - lower)).astype(BF16)

    owners = CHUNK // size
    columns = QUAD * row_count

    def term(o):
        rows = kg_out.at[pl.ds(pl.multiple_of(o * size, size), size), :]
        return remote(rows, got.at[me], ks.at[o], kr.at[me], {"seq": o})

    for i, m in enumerate(chunks):
        part = slope[m, :]
        tiled = jnp.concatenate([part] * QUAD, axis=1)
        acc = None
        for q in range(quads):
            edge = jnp.where(signs[q, m, :] > 0, tiled, 0).astype(BF16)
            signs[q, m, :] = edge
            t = jnp.dot(edge, wiq[q * columns : (q + 1) * columns, :], preferred_element_type=F32)
            acc = t if acc is None else acc + t
        acc = acc * dot_scale
        kg_all[m, :] = acc
        kg_out[m, :] = acc.astype(BF16)
        for o in range(i * owners, (i + 1) * owners):

            @pl.when(o < me)
            def _(o=o):
                term(o).start()

    def query_quad(q, _):
        base = pl.multiple_of(q * QUAD, QUAD)
        grad = jnp.dot(ikt[...], signs[q], preferred_element_type=F32)
        dots = jnp.sum(grad * iqt[q].astype(F32), axis=0, keepdims=True) * (dot_scale * head_scale)
        w = w_ref[pl.ds(base, QUAD), :] * (head_scale * dot_scale)
        for j in range(QUAD):
            cols = slice(j * row_count, (j + 1) * row_count)
            wgrad_ref[pl.ds(base + j, 1), :] = dots[:, cols]
            wide[pl.ds(base + j, row_count, stride=gheads), :] = (grad[:, cols] * w[j : j + 1]).T
        return 0

    lax.fori_loop(0, quads // 2, query_quad, 0)

    def collect(i, acc):
        remote(kg_out.at[pl.ds(0, size), :], got.at[i], ks.at[i], kr.at[i], {"seq": i}).wait_recv()
        return acc + got[i].astype(F32)

    mine[...] = lax.fori_loop(me + 1, n, collect, kg_all[pl.ds(pl.multiple_of(me * size, size), size), :])
    for k, to in enumerate(head_peers):
        sent.append(remote(mine, peer.at[k], hs.at[k], hr.at[k], {"head": to}))
        sent[-1].start()
    lax.fori_loop(quads // 2, quads, query_quad, 0)
    qgrad_ref[...] = wide[...].astype(BF16)
    acc = mine[...]
    for k in range(nh - 1):
        remote(mine, peer.at[k], hs.at[k], hr.at[k], {"head": head_peers[k]}).wait_recv()
        acc = acc + peer[k]
    kgrad_ref[...] = acc

    def settle(o, _):
        term(o).wait_send()
        return 0

    lax.fori_loop(0, me, settle, 0)
    gi.drain()
    gl.drain()
    for copy in sent:
        copy.wait_send()


def body(n, nh, latent_queries, latent_keys, index_queries, index_keys, head_weights, visible):
    row_count, gheads, depth = index_queries.shape
    heads, width = latent_queries.shape[1:]
    size = latent_keys.shape[0]
    key_count = n * size
    half = row_count // 2
    quads = gheads // QUAD
    nz, ny = line_sizes(n)
    dma = pltpu.SemaphoreType.DMA
    parts = 8
    whole = pl.BlockSpec(memory_space=VMEM)
    hbm = pl.BlockSpec(memory_space=pl.ANY)
    hops = [dma((nz,)), dma((nz,)), dma((nz, ny)), dma((nz, ny)), dma((nz, ny)), dma((nz, ny))]
    query_grad, weight_grad, key_grad = pl.pallas_call(
        functools.partial(kernel, n, nh),
        out_shape=(
            jax.ShapeDtypeStruct((row_count * gheads, depth), BF16),
            jax.ShapeDtypeStruct((gheads, row_count), F32),
            jax.ShapeDtypeStruct((size, depth), F32),
        ),
        in_specs=[whole, whole, whole, whole, hbm, hbm],
        out_specs=(whole, whole, whole),
        scratch_shapes=[
            VMEM((heads, width, row_count), BF16),
            VMEM((row_count * gheads, depth), BF16),
            VMEM((row_count * gheads, depth), F32),
            VMEM((quads, depth, QUAD * row_count), BF16),
            VMEM((gheads * row_count, depth), BF16),
            VMEM((key_count, width), BF16),
            VMEM((key_count, depth), BF16),
            VMEM((depth, key_count), BF16),
            VMEM((key_count, width + half), BF16),
            VMEM((half, LANES), BF16),
            VMEM((key_count, row_count), F32),
            VMEM((2, key_count, LANES), F32),
            VMEM((2, key_count, LANES), F32),
            VMEM((quads, key_count, QUAD * row_count), BF16),
            VMEM((key_count, row_count), F32),
            VMEM((nh - 1, key_count, row_count), F32),
            VMEM((2, key_count // 2, row_count), BF16),
            VMEM((nh - 1, 2, key_count // 2, row_count), BF16),
            VMEM((key_count, row_count), BF16),
            VMEM((2, key_count // 2, row_count), F32),
            VMEM((key_count, depth), F32),
            VMEM((key_count, depth), BF16),
            VMEM((n, size, depth), BF16),
            VMEM((size, depth), F32),
            VMEM((nh - 1, size, depth), F32),
            dma((parts,)), dma, dma((2,)), *hops, *hops,
            dma((nh - 1,)), dma((nh - 1,)), dma((nh - 1, 2)), dma((nh - 1, 2)),
            dma((n,)), dma((n,)), dma((nh - 1,)), dma((nh - 1,)),
        ],
        compiler_params=pltpu.CompilerParams(
            collective_id=0, has_side_effects=True, vmem_limit_bytes=58 * 2**20
        ),
        name="indexer_warmup",
    )(
        latent_keys, index_keys, head_weights.T, visible.reshape(1, row_count),
        jnp.transpose(latent_queries, (1, 2, 0)), index_queries.reshape(row_count * gheads, depth),
    )
    return query_grad.reshape(row_count, gheads, depth), weight_grad.T, key_grad


def solution(mesh):
    placed = (
        P("seq", "head", None),
        P("seq", None),
        P("seq", "head", None),
        P("seq", None),
        P("seq", "head"),
        P("seq"),
    )
    return jax.shard_map(
        functools.partial(body, mesh.shape["seq"], mesh.shape["head"]),
        mesh=mesh,
        in_specs=placed,
        out_specs=(P("seq", "head", None), P("seq", "head"), P("seq", None)),
        check_vma=False,
    )
```

```python
import functools
import jax
import jax.numpy as jnp
from jax import lax
from jax.experimental import pallas as pl
from jax.experimental.pallas import tpu as pltpu
from jax.sharding import PartitionSpec as P

MLA_HEADS = 128
INDEX_HEADS = 64
LOG2E = 1.4426950408889634

mla_scale = 192.0 ** (-0.5)
loss_weight = 16.0
neg_fill = -1e30
MESH = pl.DeviceIdType.MESH
VMEM = pltpu.VMEM
BF16 = jnp.bfloat16
F32 = jnp.float32
LANES = 256
CHUNK = 256
QUAD = 4


def line_sizes(n):
    ny = 2 if n <= 16 else 4
    return n // (2 * ny), ny


def remote(src, dst, ssem, rsem, device):
    return pltpu.make_async_remote_copy(
        src_ref=src, dst_ref=dst, send_sem=ssem, recv_sem=rsem, device_id=device, device_id_type=MESH
    )


class Gather:
    def __init__(self, n, ref, everything, lsem, zs, zr, ys, yr, cs, cr):
        self.nz, self.ny = line_sizes(n)
        self.me = lax.axis_index("seq")
        self.core = self.me % 2
        self.y = (self.me // 2) % self.ny
        self.z = self.me // (2 * self.ny)
        self.ref, self.everything = ref, everything
        self.size = ref.shape[0]
        self.lsem, self.zs, self.zr, self.ys, self.yr, self.cs, self.cr = lsem, zs, zr, ys, yr, cs, cr
        self.pending = []

    def at(self, zz, yy, cc):
        return (zz * self.ny + yy) * 2 + cc

    def rows(self, owner):
        return self.everything.at[pl.ds(pl.multiple_of(owner * self.size, self.size), self.size), :]

    def send(self, owner, device, ssem, rsem, first=False):
        src = self.ref if first else self.rows(owner)
        copy = remote(src, self.rows(owner), ssem, rsem, {"seq": device})
        copy.start()
        self.pending.append(copy)

    def receive(self, owner, ssem, rsem):
        remote(self.ref, self.rows(owner), ssem, rsem, {"seq": self.at(self.z, self.y, 1 - self.core)}).wait_recv()

    def keep(self):
        self.local = pltpu.make_async_copy(self.ref, self.rows(self.me), self.lsem)
        self.local.start()

    def start(self):
        z, y, core, nz, ny = self.z, self.y, self.core, self.nz, self.ny
        for k in range(1, nz):
            self.send(self.me, self.at((z + k) % nz, y, core), self.zs.at[k], self.zr.at[k], True)
        for j in range(1, ny):
            self.send(self.me, self.at(z, (y + j) % ny, core), self.ys.at[0, j], self.yr.at[0, j], True)
        self.send(self.me, self.at(z, y, 1 - core), self.cs.at[0, 0], self.cr.at[0, 0], True)

    def pass_z(self, k):
        z, y, core, nz, ny = self.z, self.y, self.core, self.nz, self.ny
        owner = self.at((z - k + nz) % nz, y, core)
        self.receive(owner, self.zs.at[k], self.zr.at[k])
        for j in range(1, ny):
            self.send(owner, self.at(z, (y + j) % ny, core), self.ys.at[k, j], self.yr.at[k, j])
        self.send(owner, self.at(z, y, 1 - core), self.cs.at[k, 0], self.cr.at[k, 0])

    def pass_y(self, k):
        z, y, core, nz, ny = self.z, self.y, self.core, self.nz, self.ny
        for j in range(1, ny):
            owner = self.at((z - k + nz) % nz, (y - j + ny) % ny, core)
            self.receive(owner, self.ys.at[k, j], self.yr.at[k, j])
            self.send(owner, self.at(z, y, 1 - core), self.cs.at[k, j], self.cr.at[k, j])

    def finish(self):
        z, y, core, nz, ny = self.z, self.y, self.core, self.nz, self.ny
        for k in range(nz):
            for j in range(ny):
                owner = self.at((z - k + nz) % nz, (y - j + ny) % ny, 1 - core)
                self.receive(owner, self.cs.at[k, j], self.cr.at[k, j])
        self.local.wait()

    def drain(self):
        for copy in self.pending:
            copy.wait_send()


def kernel(
    n, nh, lat_ref, idx_ref, w_ref, vis_ref, latq_hbm, iq_hbm,
    qgrad_hbm, wgrad_ref, kgrad_ref,
    latq, iqraw, wide, iqt, wiq, lat_all, idx_all, ikt, kaug, eye, total, sbuf, ebuf, signs,
    logit, logit_got, part_out, part_got, slope, fold, kg_all, kg_out, got, mine, peer,
    qsem, isem, osem, glsem, zs0, zr0, ys0, yr0, cs0, cr0, zs1, zr1, ys1, yr1, cs1, cr1,
    lgs, lgr, ps, pr, ks, kr, hs, hr,
):
    me = lax.axis_index("seq")
    head = lax.axis_index("head")
    heads, width, row_count = latq.shape
    key_count = lat_all.shape[0]
    depth = idx_ref.shape[1]
    gheads = w_ref.shape[0]
    size = idx_ref.shape[0]
    half = row_count // 2
    dot_scale = float(depth) ** (-0.5)
    head_scale = INDEX_HEADS ** (-0.5)
    nz, ny = line_sizes(n)

    barrier = pltpu.get_barrier_semaphore()
    for k in range(1, n):
        pl.semaphore_signal(barrier, inc=1, device_id={"seq": (me + k) % n}, device_id_type=MESH)
    for k in range(1, nh):
        pl.semaphore_signal(barrier, inc=1, device_id={"head": (head + k) % nh}, device_id_type=MESH)
    load_iq = pltpu.make_async_copy(iq_hbm, iqraw, isem)
    load_iq.start()
    parts = qsem.shape[0]
    per = heads // parts
    loads = [
        pltpu.make_async_copy(latq_hbm.at[pl.ds(i * per, per)], latq.at[pl.ds(i * per, per)], qsem.at[i])
        for i in range(parts)
    ]
    for c in loads:
        c.start()
    gi = Gather(n, idx_ref, idx_all, glsem.at[0], zs0, zr0, ys0, yr0, cs0, cr0)
    gl = Gather(n, lat_ref, lat_all, glsem.at[1], zs1, zr1, ys1, yr1, cs1, cr1)
    gi.keep()
    gl.keep()
    pl.semaphore_wait(barrier, n - 1 + nh - 1)
    gi.start()
    gl.start()

    load_iq.wait()
    wide[...] = iqraw[...].astype(F32)
    wcol = (w_ref[...] * head_scale).T

    for g in range(gheads):
        a = wide[pl.ds(g, row_count, stride=gheads), :]
        iqt[g // QUAD, :, (g % QUAD) * row_count : (g % QUAD + 1) * row_count] = a.T.astype(BF16)
        wiq[pl.ds(g * row_count, row_count), :] = (a * wcol[:, g : g + 1]).astype(BF16)
    first = lax.broadcasted_iota(jnp.int32, (half, LANES), 0)
    second = lax.broadcasted_iota(jnp.int32, (half, LANES), 1)
    eye[...] = jnp.where(first == second % half, 1.0, 0.0).astype(BF16)

    for k in range(1, nz):
        gi.pass_z(k)
    for k in range(nz):
        gi.pass_y(k)
    gi.finish()
    ikt[...] = idx_all[...].astype(F32).T.astype(BF16)
    logit[...] = jnp.zeros_like(logit)

    chunks = [slice(m, m + CHUNK) for m in range(0, key_count, CHUNK)]
    quads = gheads // QUAD

    def index_quad(q, _):
        w = w_ref[pl.ds(pl.multiple_of(q * QUAD, QUAD), QUAD), :] * (head_scale * dot_scale)
        queries = iqt[q]
        for m in chunks:
            p = jnp.dot(idx_all[m, :], queries, preferred_element_type=F32)
            signs[q, m, :] = p.astype(BF16)
            added = None
            for j in range(QUAD):
                x = jnp.maximum(p[:, j * row_count : (j + 1) * row_count], 0.0) * w[j : j + 1]
                added = x if added is None else added + x
            logit[m, :] += added
        return 0

    events = [functools.partial(gl.pass_z, k) for k in range(1, nz)]
    events += [functools.partial(gl.pass_y, k) for k in range(nz)]
    last = events.pop()
    done = 0
    for event in events:
        event()
        if done < quads:
            index_quad(done, 0)
            done += 1
    lax.fori_loop(done, quads, index_quad, 0)
    head_peers = [(head + k) % nh for k in range(1, nh)]
    sent = []
    for k, to in enumerate(head_peers):
        sent.append(remote(logit, logit_got.at[k], lgs.at[k], lgr.at[k], {"head": to}))
        sent[-1].start()
    last()
    gl.finish()
    for c in loads:
        c.wait()

    c2 = mla_scale * LOG2E
    group = LANES // half
    groups = heads // group
    kaug[:, :width] = lat_all[...]
    lane = lax.broadcasted_iota(jnp.int32, (key_count // 2, row_count), 1)
    for r in range(2):
        r0 = r * half
        ids = lax.broadcasted_iota(jnp.int32, (key_count, half), 0)
        kaug[:, width:] = jnp.where(ids < vis_ref[:, r0 : r0 + half], 0.0, neg_fill).astype(BF16)
        total[...] = jnp.zeros_like(total)

        def step(g, slot, peak, inv, r0=r0):
            if g is not None:
                several = [latq[g * group + i][:, r0 : r0 + half] for i in range(group)]
                queries = jnp.concatenate([jnp.concatenate(several, axis=1), eye[...]], axis=0)
            high = low = None
            for m in chunks:
                if inv is not None:
                    t = ebuf[slot, m, :] * inv
                    total[m, :] += t[:, : LANES // 2] + t[:, LANES // 2 :]
                if g is not None:
                    s = jnp.dot(kaug[m, :], queries, preferred_element_type=F32)
                    sbuf[slot, m, :] = s
                    t = jnp.max(s.reshape(-1, 8, LANES), axis=0)
                    high = t if high is None else jnp.maximum(high, t)
                if peak is not None:
                    e = jnp.exp2((sbuf[1 - slot, m, :] - peak) * c2)
                    ebuf[1 - slot, m, :] = e
                    t = jnp.sum(e.reshape(-1, 8, LANES), axis=0)
                    low = t if low is None else low + t
            next_peak = None if g is None else jnp.max(high, axis=0, keepdims=True)
            next_inv = None if peak is None else (1.0 / MLA_HEADS) / jnp.sum(low, axis=0, keepdims=True)
            return next_peak, next_inv

        peak, _ = step(0, 0, None, None)
        peak, inv = step(1, 1, peak, None)

        def two(i, carry):
            carry = step(2 * i + 2, 0, *carry)
            return step(2 * i + 3, 1, *carry)

        peak, inv = lax.fori_loop(0, groups // 2 - 1, two, (peak, inv))
        _, inv = step(None, 0, peak, inv)
        step(None, 1, None, inv)

        t = total[...]
        t = t + pltpu.roll(t, half, 1)
        folded = jnp.where(lane < half, t[: key_count // 2], t[key_count // 2 :])
        fold[r] = folded
        part_out[r] = folded.astype(BF16)
        for k, to in enumerate(head_peers):
            sent.append(remote(part_out.at[r], part_got.at[k, r], ps.at[k, r], pr.at[k, r], {"head": to}))
            sent[-1].start()

    for k in range(nh - 1):
        remote(logit, logit_got.at[k], lgs.at[k], lgr.at[k], {"head": head_peers[k]}).wait_recv()
    both = logit[...]
    for k in range(nh - 1):
        both = both + logit_got[k]
    ids = lax.broadcasted_iota(jnp.int32, (key_count, row_count), 0)
    both = jnp.where(ids < vis_ref[...], both, neg_fill)
    weights = jnp.exp(both - jnp.max(both, axis=0, keepdims=True))
    total[...] = weights * (1.0 / jnp.sum(weights, axis=0, keepdims=True))
    folds = []
    for r in range(2):
        t = fold[r]
        for k in range(nh - 1):
            remote(part_out.at[r], part_got.at[k, r], ps.at[k, r], pr.at[k, r], {"head": head_peers[k]}).wait_recv()
            t = t + part_got[k, r].astype(F32)
        folds.append(t)
    upper = jnp.where(lane < half, folds[0], pltpu.roll(folds[1], half, 1))
    lower = jnp.where(lane < half, pltpu.roll(folds[0], half, 1), folds[1])
    slope[: key_count // 2, :] = (loss_weight * (total[: key_count // 2, :] - upper)).astype(BF16)
    slope[key_count // 2 :, :] = (loss_weight * (total[key_count // 2 :, :] - lower)).astype(BF16)

    owners = CHUNK // size
    columns = QUAD * row_count

    def term(o):
        rows = kg_out.at[pl.ds(pl.multiple_of(o * size, size), size), :]
        return remote(rows, got.at[me], ks.at[o], kr.at[me], {"seq": o})

    for i, m in enumerate(chunks):
        part = slope[m, :]
        tiled = jnp.concatenate([part] * QUAD, axis=1)
        acc = None
        for q in range(quads):
            edge = jnp.where(signs[q, m, :] > 0, tiled, 0).astype(BF16)
            signs[q, m, :] = edge
            t = jnp.dot(edge, wiq[q * columns : (q + 1) * columns, :], preferred_element_type=F32)
            acc = t if acc is None else acc + t
        acc = acc * dot_scale
        kg_all[m, :] = acc
        kg_out[m, :] = acc.astype(BF16)
        for o in range(i * owners, (i + 1) * owners):

            @pl.when(o < me)
            def _(o=o):
                term(o).start()

    def query_quad(q, _):
        base = pl.multiple_of(q * QUAD, QUAD)
        grad = jnp.dot(ikt[...], signs[q], preferred_element_type=F32)
        dots = jnp.sum(grad * iqt[q].astype(F32), axis=0, keepdims=True) * (dot_scale * head_scale)
        w = w_ref[pl.ds(base, QUAD), :] * (head_scale * dot_scale)
        for j in range(QUAD):
            cols = slice(j * row_count, (j + 1) * row_count)
            wgrad_ref[pl.ds(base + j, 1), :] = dots[:, cols]
            wide[pl.ds(base + j, row_count, stride=gheads), :] = (grad[:, cols] * w[j : j + 1]).T
        return 0

    lax.fori_loop(0, quads // 2, query_quad, 0)

    def collect(i, acc):
        remote(kg_out.at[pl.ds(0, size), :], got.at[i], ks.at[i], kr.at[i], {"seq": i}).wait_recv()
        return acc + got[i].astype(F32)

    mine[...] = lax.fori_loop(me + 1, n, collect, kg_all[pl.ds(pl.multiple_of(me * size, size), size), :])
    for k, to in enumerate(head_peers):
        sent.append(remote(mine, peer.at[k], hs.at[k], hr.at[k], {"head": to}))
        sent[-1].start()
    lax.fori_loop(quads // 2, quads, query_quad, 0)
    iqraw[...] = wide[...].astype(BF16)
    store = pltpu.make_async_copy(iqraw, qgrad_hbm, osem)
    store.start()
    acc = mine[...]
    for k in range(nh - 1):
        remote(mine, peer.at[k], hs.at[k], hr.at[k], {"head": head_peers[k]}).wait_recv()
        acc = acc + peer[k]
    kgrad_ref[...] = acc

    def settle(o, _):
        term(o).wait_send()
        return 0

    lax.fori_loop(0, me, settle, 0)
    gi.drain()
    gl.drain()
    for copy in sent:
        copy.wait_send()
    store.wait()


def deliver_kernel(*refs):
    count = (len(refs) - 1) // 2
    copies = [pltpu.make_async_copy(refs[i], refs[count + i], refs[-1].at[i]) for i in range(count)]
    for copy in copies:
        copy.start()
    for copy in copies:
        copy.wait()


def deliver(*arrays):
    hbm = pl.BlockSpec(memory_space=pl.ANY)
    return pl.pallas_call(
        deliver_kernel,
        out_shape=tuple(jax.ShapeDtypeStruct(a.shape, a.dtype) for a in arrays),
        in_specs=[hbm] * len(arrays),
        out_specs=(hbm,) * len(arrays),
        scratch_shapes=[pltpu.SemaphoreType.DMA((len(arrays),))],
        name="deliver",
    )(*arrays)


def body(n, nh, latent_queries, latent_keys, index_queries, index_keys, head_weights, visible):
    row_count, gheads, depth = index_queries.shape
    heads, width = latent_queries.shape[1:]
    size = latent_keys.shape[0]
    key_count = n * size
    half = row_count // 2
    quads = gheads // QUAD
    nz, ny = line_sizes(n)
    dma = pltpu.SemaphoreType.DMA
    parts = 8
    whole = pl.BlockSpec(memory_space=VMEM)
    hbm = pl.BlockSpec(memory_space=pl.ANY)
    hops = [dma((nz,)), dma((nz,)), dma((nz, ny)), dma((nz, ny)), dma((nz, ny)), dma((nz, ny))]
    query_grad, weight_grad, key_grad = pl.pallas_call(
        functools.partial(kernel, n, nh),
        out_shape=(
            jax.ShapeDtypeStruct((row_count * gheads, depth), BF16),
            jax.ShapeDtypeStruct((gheads, row_count), F32),
            jax.ShapeDtypeStruct((size, depth), F32),
        ),
        in_specs=[whole, whole, whole, whole, hbm, hbm],
        out_specs=(hbm, whole, whole),
        scratch_shapes=[
            VMEM((heads, width, row_count), BF16),
            VMEM((row_count * gheads, depth), BF16),
            VMEM((row_count * gheads, depth), F32),
            VMEM((quads, depth, QUAD * row_count), BF16),
            VMEM((gheads * row_count, depth), BF16),
            VMEM((key_count, width), BF16),
            VMEM((key_count, depth), BF16),
            VMEM((depth, key_count), BF16),
            VMEM((key_count, width + half), BF16),
            VMEM((half, LANES), BF16),
            VMEM((key_count, row_count), F32),
            VMEM((2, key_count, LANES), F32),
            VMEM((2, key_count, LANES), F32),
            VMEM((quads, key_count, QUAD * row_count), BF16),
            VMEM((key_count, row_count), F32),
            VMEM((nh - 1, key_count, row_count), F32),
            VMEM((2, key_count // 2, row_count), BF16),
            VMEM((nh - 1, 2, key_count // 2, row_count), BF16),
            VMEM((key_count, row_count), BF16),
            VMEM((2, key_count // 2, row_count), F32),
            VMEM((key_count, depth), F32),
            VMEM((key_count, depth), BF16),
            VMEM((n, size, depth), BF16),
            VMEM((size, depth), F32),
            VMEM((nh - 1, size, depth), F32),
            dma((parts,)), dma, dma, dma((2,)), *hops, *hops,
            dma((nh - 1,)), dma((nh - 1,)), dma((nh - 1, 2)), dma((nh - 1, 2)),
            dma((n,)), dma((n,)), dma((nh - 1,)), dma((nh - 1,)),
        ],
        compiler_params=pltpu.CompilerParams(
            collective_id=0, has_side_effects=True, vmem_limit_bytes=58 * 2**20
        ),
        name="indexer_warmup",
    )(
        latent_keys, index_keys, head_weights.T, visible.reshape(1, row_count),
        jnp.transpose(latent_queries, (1, 2, 0)), index_queries.reshape(row_count * gheads, depth),
    )
    query_grad, weight_grad, key_grad = deliver(query_grad, weight_grad, key_grad)
    return query_grad.reshape(row_count, gheads, depth), weight_grad.T, key_grad


def solution(mesh):
    placed = (
        P("seq", "head", None),
        P("seq", None),
        P("seq", "head", None),
        P("seq", None),
        P("seq", "head"),
        P("seq"),
    )
    return jax.shard_map(
        functools.partial(body, mesh.shape["seq"], mesh.shape["head"]),
        mesh=mesh,
        in_specs=placed,
        out_specs=(P("seq", "head", None), P("seq", "head"), P("seq", None)),
        check_vma=False,
    )
```

```python
import functools
import jax
import jax.numpy as jnp
from jax import lax
from jax.experimental import pallas as pl
from jax.experimental.pallas import tpu as pltpu
from jax.sharding import PartitionSpec as P

MLA_HEADS = 128
INDEX_HEADS = 64
LOG2E = 1.4426950408889634

mla_scale = 192.0 ** (-0.5)
loss_weight = 16.0
neg_fill = -1e30
MESH = pl.DeviceIdType.MESH
VMEM = pltpu.VMEM
BF16 = jnp.bfloat16
F32 = jnp.float32
LANES = 256
CHUNK = 256
QUAD = 4
PIECES = 2
BLOCK = 128


def line_sizes(n):
    ny = 2 if n <= 16 else 4
    return n // (2 * ny), ny


def remote(src, dst, ssem, rsem, device):
    return pltpu.make_async_remote_copy(
        src_ref=src, dst_ref=dst, send_sem=ssem, recv_sem=rsem, device_id=device, device_id_type=MESH
    )


class Gather:
    def __init__(self, n, ref, everything, lsem, zs, zr, ys, yr, cs, cr, piece=0, pieces=1):
        self.nz, self.ny = line_sizes(n)
        self.me = lax.axis_index("seq")
        self.core = self.me % 2
        self.y = (self.me // 2) % self.ny
        self.z = self.me // (2 * self.ny)
        self.full = ref.shape[0]
        self.size = self.full // pieces
        self.offset = piece * self.size
        self.ref, self.everything = ref.at[pl.ds(self.offset, self.size), :], everything
        self.lsem, self.zs, self.zr, self.ys, self.yr, self.cs, self.cr = lsem, zs, zr, ys, yr, cs, cr
        self.pending = []

    def at(self, zz, yy, cc):
        return (zz * self.ny + yy) * 2 + cc

    def rows(self, owner):
        start = pl.multiple_of(owner * self.full + self.offset, self.size)
        return self.everything.at[pl.ds(start, self.size), :]

    def send(self, owner, device, ssem, rsem, first=False):
        src = self.ref if first else self.rows(owner)
        copy = remote(src, self.rows(owner), ssem, rsem, {"seq": device})
        copy.start()
        self.pending.append(copy)

    def receive(self, owner, ssem, rsem):
        remote(self.ref, self.rows(owner), ssem, rsem, {"seq": self.at(self.z, self.y, 1 - self.core)}).wait_recv()

    def keep(self):
        self.local = pltpu.make_async_copy(self.ref, self.rows(self.me), self.lsem)
        self.local.start()

    def start(self):
        z, y, core, nz, ny = self.z, self.y, self.core, self.nz, self.ny
        for k in range(1, nz):
            self.send(self.me, self.at((z + k) % nz, y, core), self.zs.at[k], self.zr.at[k], True)
        for j in range(1, ny):
            self.send(self.me, self.at(z, (y + j) % ny, core), self.ys.at[0, j], self.yr.at[0, j], True)
        self.send(self.me, self.at(z, y, 1 - core), self.cs.at[0, 0], self.cr.at[0, 0], True)

    def pass_z(self, k):
        z, y, core, nz, ny = self.z, self.y, self.core, self.nz, self.ny
        owner = self.at((z - k + nz) % nz, y, core)
        self.receive(owner, self.zs.at[k], self.zr.at[k])
        for j in range(1, ny):
            self.send(owner, self.at(z, (y + j) % ny, core), self.ys.at[k, j], self.yr.at[k, j])
        self.send(owner, self.at(z, y, 1 - core), self.cs.at[k, 0], self.cr.at[k, 0])

    def pass_y(self, k):
        z, y, core, nz, ny = self.z, self.y, self.core, self.nz, self.ny
        for j in range(1, ny):
            owner = self.at((z - k + nz) % nz, (y - j + ny) % ny, core)
            self.receive(owner, self.ys.at[k, j], self.yr.at[k, j])
            self.send(owner, self.at(z, y, 1 - core), self.cs.at[k, j], self.cr.at[k, j])

    def finish(self):
        z, y, core, nz, ny = self.z, self.y, self.core, self.nz, self.ny
        for k in range(nz):
            for j in range(ny):
                owner = self.at((z - k + nz) % nz, (y - j + ny) % ny, 1 - core)
                self.receive(owner, self.cs.at[k, j], self.cr.at[k, j])
        self.local.wait()

    def drain(self):
        for copy in self.pending:
            copy.wait_send()


def kernel(
    n, nh, lat_ref, idx_ref, w_ref, vis_ref, latq_hbm, iq_hbm,
    qgrad_hbm, wgrad_ref, kgrad_ref,
    latq, iqraw, wide, iqt, wiq, lat_all, idx_all, ikt, kaug, eye, total, ebuf, signs,
    logit, logit_got, part_out, part_got, slope, fold, kg_all, kg_out, got, mine, peer,
    qsem, isem, osem, glsem, zs0, zr0, ys0, yr0, cs0, cr0, *hops,
):
    lgs, lgr, ps, pr, ks, kr, hs, hr = hops[6 * PIECES :]
    me = lax.axis_index("seq")
    head = lax.axis_index("head")
    heads, width, row_count = latq.shape
    key_count = lat_all.shape[0]
    depth = idx_ref.shape[1]
    gheads = w_ref.shape[0]
    size = idx_ref.shape[0]
    half = row_count // 2
    dot_scale = float(depth) ** (-0.5)
    head_scale = INDEX_HEADS ** (-0.5)
    nz, ny = line_sizes(n)

    barrier = pltpu.get_barrier_semaphore()
    for k in range(1, n):
        pl.semaphore_signal(barrier, inc=1, device_id={"seq": (me + k) % n}, device_id_type=MESH)
    for k in range(1, nh):
        pl.semaphore_signal(barrier, inc=1, device_id={"head": (head + k) % nh}, device_id_type=MESH)
    load_iq = pltpu.make_async_copy(iq_hbm, iqraw, isem)
    load_iq.start()
    parts = qsem.shape[0]
    per = heads // parts
    loads = [
        pltpu.make_async_copy(latq_hbm.at[pl.ds(i * per, per)], latq.at[pl.ds(i * per, per)], qsem.at[i])
        for i in range(parts)
    ]
    for c in loads:
        c.start()
    gi = Gather(n, idx_ref, idx_all, glsem.at[0], zs0, zr0, ys0, yr0, cs0, cr0)
    gls = [
        Gather(n, lat_ref, lat_all, glsem.at[1 + i], *hops[6 * i : 6 * i + 6], piece=i, pieces=PIECES)
        for i in range(PIECES)
    ]
    gi.keep()
    for gl in gls:
        gl.keep()
    pl.semaphore_wait(barrier, n - 1 + nh - 1)
    gi.start()
    for gl in gls:
        gl.start()

    load_iq.wait()
    wide[...] = iqraw[...].astype(F32)
    wcol = (w_ref[...] * head_scale).T

    for g in range(gheads):
        a = wide[pl.ds(g, row_count, stride=gheads), :]
        iqt[g // QUAD, :, (g % QUAD) * row_count : (g % QUAD + 1) * row_count] = a.T.astype(BF16)
        wiq[pl.ds(g * row_count, row_count), :] = (a * wcol[:, g : g + 1]).astype(BF16)
    first = lax.broadcasted_iota(jnp.int32, (half, LANES), 0)
    second = lax.broadcasted_iota(jnp.int32, (half, LANES), 1)
    eye[...] = jnp.where(first == second % half, 1.0, 0.0).astype(BF16)

    for k in range(1, nz):
        gi.pass_z(k)
    for k in range(nz):
        gi.pass_y(k)
    gi.finish()
    ikt[...] = idx_all[...].astype(F32).T.astype(BF16)
    logit[...] = jnp.zeros_like(logit)

    chunks = [slice(m, m + CHUNK) for m in range(0, key_count, CHUNK)]
    quads = gheads // QUAD

    def index_quad(q, _):
        w = w_ref[pl.ds(pl.multiple_of(q * QUAD, QUAD), QUAD), :] * (head_scale * dot_scale)
        queries = iqt[q]
        for m in chunks:
            p = jnp.dot(idx_all[m, :], queries, preferred_element_type=F32)
            signs[q, m, :] = p.astype(BF16)
            added = None
            for j in range(QUAD):
                x = jnp.maximum(p[:, j * row_count : (j + 1) * row_count], 0.0) * w[j : j + 1]
                added = x if added is None else added + x
            logit[m, :] += added
        return 0

    events = []
    for gl in gls:
        events += [functools.partial(gl.pass_z, k) for k in range(1, nz)]
    for gl in gls:
        events += [functools.partial(gl.pass_y, k) for k in range(nz)]
    last = events.pop()
    done = 0
    for event in events:
        event()
        if done < quads:
            index_quad(done, 0)
            done += 1
    lax.fori_loop(done, quads, index_quad, 0)
    head_peers = [(head + k) % nh for k in range(1, nh)]
    sent = []
    for k, to in enumerate(head_peers):
        sent.append(remote(logit, logit_got.at[k], lgs.at[k], lgr.at[k], {"head": to}))
        sent[-1].start()
    last()
    for gl in gls:
        gl.finish()
    for c in loads:
        c.wait()

    c2 = mla_scale * LOG2E
    group = LANES // half
    blocks = [slice(m, m + BLOCK) for m in range(0, key_count, BLOCK)]
    groups = heads // group
    kaug[:, :width] = lat_all[...]
    lane = lax.broadcasted_iota(jnp.int32, (key_count // 2, row_count), 1)
    for r in range(2):
        r0 = r * half
        ids = lax.broadcasted_iota(jnp.int32, (key_count, half), 0)
        kaug[:, width:] = jnp.where(ids < vis_ref[:, r0 : r0 + half], 0.0, neg_fill).astype(BF16)
        total[...] = jnp.zeros_like(total)

        def step(g, slot, factors, r0=r0):
            if g is not None:
                several = [latq[g * group + i][:, r0 : r0 + half] for i in range(group)]
                queries = jnp.concatenate([jnp.concatenate(several, axis=1), eye[...]], axis=0)
            peaks, sums = [], []
            for i, m in enumerate(blocks):
                if factors is not None:
                    t = ebuf[1 - slot, m, :] * factors[i]
                    total[m, :] += t[:, : LANES // 2] + t[:, LANES // 2 :]
                if g is not None:
                    s = jnp.dot(kaug[m, :], queries, preferred_element_type=F32)
                    peak = jnp.max(s, axis=0, keepdims=True)
                    e = jnp.exp2((s - peak) * c2)
                    ebuf[slot, m, :] = e
                    peaks.append(peak)
                    sums.append(jnp.sum(e, axis=0, keepdims=True))
            if g is None:
                return None
            highest = functools.reduce(jnp.maximum, peaks)
            scales = [jnp.exp2((peak - highest) * c2) for peak in peaks]
            inv = (1.0 / MLA_HEADS) / sum(f * x for f, x in zip(scales, sums))
            return tuple(f * inv for f in scales)

        factors = step(0, 0, None)

        def two(i, carry):
            return step(2 * i + 2, 0, step(2 * i + 1, 1, carry))

        factors = lax.fori_loop(0, groups // 2 - 1, two, factors)
        factors = step(groups - 1, 1, factors)
        step(None, 0, factors)

        t = total[...]
        t = t + pltpu.roll(t, half, 1)
        folded = jnp.where(lane < half, t[: key_count // 2], t[key_count // 2 :])
        fold[r] = folded
        part_out[r] = folded.astype(BF16)
        for k, to in enumerate(head_peers):
            sent.append(remote(part_out.at[r], part_got.at[k, r], ps.at[k, r], pr.at[k, r], {"head": to}))
            sent[-1].start()

    for k in range(nh - 1):
        remote(logit, logit_got.at[k], lgs.at[k], lgr.at[k], {"head": head_peers[k]}).wait_recv()
    both = logit[...]
    for k in range(nh - 1):
        both = both + logit_got[k]
    ids = lax.broadcasted_iota(jnp.int32, (key_count, row_count), 0)
    both = jnp.where(ids < vis_ref[...], both, neg_fill)
    weights = jnp.exp(both - jnp.max(both, axis=0, keepdims=True))
    total[...] = weights * (1.0 / jnp.sum(weights, axis=0, keepdims=True))
    folds = []
    for r in range(2):
        t = fold[r]
        for k in range(nh - 1):
            remote(part_out.at[r], part_got.at[k, r], ps.at[k, r], pr.at[k, r], {"head": head_peers[k]}).wait_recv()
            t = t + part_got[k, r].astype(F32)
        folds.append(t)
    upper = jnp.where(lane < half, folds[0], pltpu.roll(folds[1], half, 1))
    lower = jnp.where(lane < half, pltpu.roll(folds[0], half, 1), folds[1])
    slope[: key_count // 2, :] = (loss_weight * (total[: key_count // 2, :] - upper)).astype(BF16)
    slope[key_count // 2 :, :] = (loss_weight * (total[key_count // 2 :, :] - lower)).astype(BF16)

    owners = CHUNK // size
    columns = QUAD * row_count

    def term(o):
        rows = kg_out.at[pl.ds(pl.multiple_of(o * size, size), size), :]
        return remote(rows, got.at[me], ks.at[o], kr.at[me], {"seq": o})

    for i, m in enumerate(chunks):
        part = slope[m, :]
        tiled = jnp.concatenate([part] * QUAD, axis=1)
        acc = None
        for q in range(quads):
            edge = jnp.where(signs[q, m, :] > 0, tiled, 0).astype(BF16)
            signs[q, m, :] = edge
            t = jnp.dot(edge, wiq[q * columns : (q + 1) * columns, :], preferred_element_type=F32)
            acc = t if acc is None else acc + t
        acc = acc * dot_scale
        kg_all[m, :] = acc
        kg_out[m, :] = acc.astype(BF16)
        for o in range(i * owners, (i + 1) * owners):

            @pl.when(o < me)
            def _(o=o):
                term(o).start()

    def query_quad(q, _):
        base = pl.multiple_of(q * QUAD, QUAD)
        grad = jnp.dot(ikt[...], signs[q], preferred_element_type=F32)
        dots = jnp.sum(grad * iqt[q].astype(F32), axis=0, keepdims=True) * (dot_scale * head_scale)
        w = w_ref[pl.ds(base, QUAD), :] * (head_scale * dot_scale)
        for j in range(QUAD):
            cols = slice(j * row_count, (j + 1) * row_count)
            wgrad_ref[pl.ds(base + j, 1), :] = dots[:, cols]
            wide[pl.ds(base + j, row_count, stride=gheads), :] = (grad[:, cols] * w[j : j + 1]).T
        return 0

    lax.fori_loop(0, quads // 2, query_quad, 0)

    def collect(i, acc):
        remote(kg_out.at[pl.ds(0, size), :], got.at[i], ks.at[i], kr.at[i], {"seq": i}).wait_recv()
        return acc + got[i].astype(F32)

    mine[...] = lax.fori_loop(me + 1, n, collect, kg_all[pl.ds(pl.multiple_of(me * size, size), size), :])
    for k, to in enumerate(head_peers):
        sent.append(remote(mine, peer.at[k], hs.at[k], hr.at[k], {"head": to}))
        sent[-1].start()
    lax.fori_loop(quads // 2, quads, query_quad, 0)
    iqraw[...] = wide[...].astype(BF16)
    store = pltpu.make_async_copy(iqraw, qgrad_hbm, osem)
    store.start()
    acc = mine[...]
    for k in range(nh - 1):
        remote(mine, peer.at[k], hs.at[k], hr.at[k], {"head": head_peers[k]}).wait_recv()
        acc = acc + peer[k]
    kgrad_ref[...] = acc

    def settle(o, _):
        term(o).wait_send()
        return 0

    lax.fori_loop(0, me, settle, 0)
    gi.drain()
    for gl in gls:
        gl.drain()
    for copy in sent:
        copy.wait_send()
    store.wait()


def deliver_kernel(*refs):
    count = len(refs) // 2
    for source, target in zip(refs[:count], refs[count:]):
        target[...] = source[...]


def deliver(*arrays, steps=4):
    specs = [pl.BlockSpec((a.shape[0] // steps, a.shape[1]), lambda i: (i, 0)) for a in arrays]
    return pl.pallas_call(
        deliver_kernel,
        out_shape=tuple(jax.ShapeDtypeStruct(a.shape, a.dtype) for a in arrays),
        grid=(steps,),
        in_specs=specs,
        out_specs=tuple(specs),
        name="deliver",
    )(*arrays)


def body(n, nh, latent_queries, latent_keys, index_queries, index_keys, head_weights, visible):
    row_count, gheads, depth = index_queries.shape
    heads, width = latent_queries.shape[1:]
    size = latent_keys.shape[0]
    key_count = n * size
    half = row_count // 2
    quads = gheads // QUAD
    nz, ny = line_sizes(n)
    dma = pltpu.SemaphoreType.DMA
    parts = 8
    whole = pl.BlockSpec(memory_space=VMEM)
    hbm = pl.BlockSpec(memory_space=pl.ANY)
    hops = [dma((nz,)), dma((nz,)), dma((nz, ny)), dma((nz, ny)), dma((nz, ny)), dma((nz, ny))]
    query_grad, weight_grad, key_grad = pl.pallas_call(
        functools.partial(kernel, n, nh),
        out_shape=(
            jax.ShapeDtypeStruct((row_count * gheads, depth), BF16),
            jax.ShapeDtypeStruct((gheads, row_count), F32),
            jax.ShapeDtypeStruct((size, depth), F32),
        ),
        in_specs=[whole, whole, whole, whole, hbm, hbm],
        out_specs=(hbm, whole, whole),
        scratch_shapes=[
            VMEM((heads, width, row_count), BF16),
            VMEM((row_count * gheads, depth), BF16),
            VMEM((row_count * gheads, depth), F32),
            VMEM((quads, depth, QUAD * row_count), BF16),
            VMEM((gheads * row_count, depth), BF16),
            VMEM((key_count, width), BF16),
            VMEM((key_count, depth), BF16),
            VMEM((depth, key_count), BF16),
            VMEM((key_count, width + half), BF16),
            VMEM((half, LANES), BF16),
            VMEM((key_count, row_count), F32),
            VMEM((2, key_count, LANES), F32),
            VMEM((quads, key_count, QUAD * row_count), BF16),
            VMEM((key_count, row_count), F32),
            VMEM((nh - 1, key_count, row_count), F32),
            VMEM((2, key_count // 2, row_count), BF16),
            VMEM((nh - 1, 2, key_count // 2, row_count), BF16),
            VMEM((key_count, row_count), BF16),
            VMEM((2, key_count // 2, row_count), F32),
            VMEM((key_count, depth), F32),
            VMEM((key_count, depth), BF16),
            VMEM((n, size, depth), BF16),
            VMEM((size, depth), F32),
            VMEM((nh - 1, size, depth), F32),
            dma((parts,)), dma, dma, dma((1 + PIECES,)), *hops, *(hops * PIECES),
            dma((nh - 1,)), dma((nh - 1,)), dma((nh - 1, 2)), dma((nh - 1, 2)),
            dma((n,)), dma((n,)), dma((nh - 1,)), dma((nh - 1,)),
        ],
        compiler_params=pltpu.CompilerParams(
            collective_id=0, has_side_effects=True, vmem_limit_bytes=58 * 2**20
        ),
        name="indexer_warmup",
    )(
        latent_keys, index_keys, head_weights.T, visible.reshape(1, row_count),
        jnp.transpose(latent_queries, (1, 2, 0)), index_queries.reshape(row_count * gheads, depth),
    )
    query_grad, weight_grad, key_grad = deliver(query_grad, weight_grad, key_grad, steps=gheads % 32 == 0 and 4 or 1)
    return query_grad.reshape(row_count, gheads, depth), weight_grad.T, key_grad


def solution(mesh):
    placed = (
        P("seq", "head", None),
        P("seq", None),
        P("seq", "head", None),
        P("seq", None),
        P("seq", "head"),
        P("seq"),
    )
    return jax.shard_map(
        functools.partial(body, mesh.shape["seq"], mesh.shape["head"]),
        mesh=mesh,
        in_specs=placed,
        out_specs=(P("seq", "head", None), P("seq", "head"), P("seq", None)),
        check_vma=False,
    )
```

```python
import functools
import jax
import jax.numpy as jnp
from jax import lax
from jax.experimental import pallas as pl
from jax.experimental.pallas import tpu as pltpu
from jax.sharding import PartitionSpec as P

MLA_HEADS = 128
INDEX_HEADS = 64
LOG2E = 1.4426950408889634

mla_scale = 192.0 ** (-0.5)
loss_weight = 16.0
neg_fill = -1e30
MESH = pl.DeviceIdType.MESH
VMEM = pltpu.VMEM
BF16 = jnp.bfloat16
F32 = jnp.float32
LANES = 256
CHUNK = 256
QUAD = 4
PIECES = 2
BLOCK = 128


def line_sizes(n):
    ny = 2 if n <= 16 else 4
    return n // (2 * ny), ny


def remote(src, dst, ssem, rsem, device):
    return pltpu.make_async_remote_copy(
        src_ref=src, dst_ref=dst, send_sem=ssem, recv_sem=rsem, device_id=device, device_id_type=MESH
    )


class Gather:
    def __init__(self, n, ref, everything, lsem, zs, zr, ys, yr, cs, cr, piece=0, pieces=1):
        self.nz, self.ny = line_sizes(n)
        self.me = lax.axis_index("seq")
        self.core = self.me % 2
        self.y = (self.me // 2) % self.ny
        self.z = self.me // (2 * self.ny)
        self.full = ref.shape[0]
        self.size = self.full // pieces
        self.offset = piece * self.size
        self.ref, self.everything = ref.at[pl.ds(self.offset, self.size), :], everything
        self.lsem, self.zs, self.zr, self.ys, self.yr, self.cs, self.cr = lsem, zs, zr, ys, yr, cs, cr
        self.pending = []

    def at(self, zz, yy, cc):
        return (zz * self.ny + yy) * 2 + cc

    def rows(self, owner):
        start = pl.multiple_of(owner * self.full + self.offset, self.size)
        return self.everything.at[pl.ds(start, self.size), :]

    def send(self, owner, device, ssem, rsem):
        copy = remote(self.rows(owner), self.rows(owner), ssem, rsem, {"seq": device})
        copy.start()
        self.pending.append(copy)

    def receive(self, owner, ssem, rsem):
        other = {"seq": self.at(self.z, self.y, 1 - self.core)}
        remote(self.rows(owner), self.rows(owner), ssem, rsem, other).wait_recv()

    def keep(self):
        self.local = pltpu.make_async_copy(self.ref, self.rows(self.me), self.lsem)
        self.local.start()

    def start(self):
        z, y, core, nz, ny = self.z, self.y, self.core, self.nz, self.ny
        self.local.wait()
        for k in range(1, nz):
            self.send(self.me, self.at((z + k) % nz, y, core), self.zs.at[k], self.zr.at[k])
        for j in range(1, ny):
            self.send(self.me, self.at(z, (y + j) % ny, core), self.ys.at[0, j], self.yr.at[0, j])
        self.send(self.me, self.at(z, y, 1 - core), self.cs.at[0, 0], self.cr.at[0, 0])

    def pass_z(self, k):
        z, y, core, nz, ny = self.z, self.y, self.core, self.nz, self.ny
        owner = self.at((z - k + nz) % nz, y, core)
        self.receive(owner, self.zs.at[k], self.zr.at[k])
        for j in range(1, ny):
            self.send(owner, self.at(z, (y + j) % ny, core), self.ys.at[k, j], self.yr.at[k, j])
        self.send(owner, self.at(z, y, 1 - core), self.cs.at[k, 0], self.cr.at[k, 0])

    def pass_y(self, k):
        z, y, core, nz, ny = self.z, self.y, self.core, self.nz, self.ny
        for j in range(1, ny):
            owner = self.at((z - k + nz) % nz, (y - j + ny) % ny, core)
            self.receive(owner, self.ys.at[k, j], self.yr.at[k, j])
            self.send(owner, self.at(z, y, 1 - core), self.cs.at[k, j], self.cr.at[k, j])

    def finish(self):
        z, y, core, nz, ny = self.z, self.y, self.core, self.nz, self.ny
        for k in range(nz):
            for j in range(ny):
                owner = self.at((z - k + nz) % nz, (y - j + ny) % ny, 1 - core)
                self.receive(owner, self.cs.at[k, j], self.cr.at[k, j])

    def drain(self):
        for copy in self.pending:
            copy.wait_send()
        self.pending = []


def kernel(
    n, nh, lat_ref, idx_ref, w_ref, vis_ref, latq_hbm, iq_hbm,
    qgrad_ref, wgrad_ref, kgrad_ref,
    latq, iqraw, wide, iqt, wiq, lat_all, idx_all, ikt, kaug, eye, total, ebuf, signs,
    logit, logit_got, part_out, part_got, slope, fold, kg_all, kg_out, got, mine, peer,
    qsem, isem, glsem, zs0, zr0, ys0, yr0, cs0, cr0, *hops,
):
    lgs, lgr, ps, pr, ks, kr, hs, hr = hops[6 * PIECES :]
    me = lax.axis_index("seq")
    head = lax.axis_index("head")
    heads, width, row_count = latq.shape
    key_count = lat_all.shape[0]
    depth = idx_ref.shape[1]
    gheads = w_ref.shape[0]
    size = idx_ref.shape[0]
    half = row_count // 2
    dot_scale = float(depth) ** (-0.5)
    head_scale = INDEX_HEADS ** (-0.5)
    nz, ny = line_sizes(n)

    barrier = pltpu.get_barrier_semaphore()
    for k in range(1, n):
        pl.semaphore_signal(barrier, inc=1, device_id={"seq": (me + k) % n}, device_id_type=MESH)
    for k in range(1, nh):
        pl.semaphore_signal(barrier, inc=1, device_id={"head": (head + k) % nh}, device_id_type=MESH)
    gi = Gather(n, idx_ref, idx_all, glsem.at[0], zs0, zr0, ys0, yr0, cs0, cr0)
    gls = [
        Gather(n, lat_ref, lat_all, glsem.at[1 + i], *hops[6 * i : 6 * i + 6], piece=i, pieces=PIECES)
        for i in range(PIECES)
    ]
    gi.keep()
    for gl in gls:
        gl.keep()
    load_iq = pltpu.make_async_copy(iq_hbm, iqraw, isem)
    load_iq.start()
    parts = qsem.shape[0]
    per = heads // parts
    loads = [
        pltpu.make_async_copy(latq_hbm.at[pl.ds(i * per, per)], latq.at[pl.ds(i * per, per)], qsem.at[i])
        for i in range(parts)
    ]
    for c in loads:
        c.start()
    pl.semaphore_wait(barrier, n - 1 + nh - 1)
    gi.start()
    gls[0].start()

    load_iq.wait()
    wide[...] = iqraw[...].astype(F32)
    wcol = (w_ref[...] * head_scale).T

    for g in range(gheads):
        a = wide[pl.ds(g, row_count, stride=gheads), :]
        iqt[g // QUAD, :, (g % QUAD) * row_count : (g % QUAD + 1) * row_count] = a.T.astype(BF16)
        wiq[pl.ds(g * row_count, row_count), :] = (a * wcol[:, g : g + 1]).astype(BF16)
    first = lax.broadcasted_iota(jnp.int32, (half, LANES), 0)
    second = lax.broadcasted_iota(jnp.int32, (half, LANES), 1)
    eye[...] = jnp.where(first == second % half, 1.0, 0.0).astype(BF16)

    for k in range(1, nz):
        gi.pass_z(k)
    gls[0].drain()
    gls[1].start()
    for k in range(nz):
        gi.pass_y(k)
    for k in range(1, nz):
        gls[0].pass_z(k)
    gi.finish()
    ikt[...] = idx_all[...].astype(F32).T.astype(BF16)
    logit[...] = jnp.zeros_like(logit)

    chunks = [slice(m, m + CHUNK) for m in range(0, key_count, CHUNK)]
    quads = gheads // QUAD

    def index_quad(q, _):
        w = w_ref[pl.ds(pl.multiple_of(q * QUAD, QUAD), QUAD), :] * (head_scale * dot_scale)
        queries = iqt[q]
        for m in chunks:
            p = jnp.dot(idx_all[m, :], queries, preferred_element_type=F32)
            signs[q, m, :] = p.astype(BF16)
            added = None
            for j in range(QUAD):
                x = jnp.maximum(p[:, j * row_count : (j + 1) * row_count], 0.0) * w[j : j + 1]
                added = x if added is None else added + x
            logit[m, :] += added
        return 0

    events = []
    for gl in gls[1:]:
        events += [functools.partial(gl.pass_z, k) for k in range(1, nz)]
    for gl in gls:
        events += [functools.partial(gl.pass_y, k) for k in range(nz)]
    last = events.pop()
    done = 0
    for event in events:
        event()
        if done < quads:
            index_quad(done, 0)
            done += 1
    lax.fori_loop(done, quads, index_quad, 0)
    head_peers = [(head + k) % nh for k in range(1, nh)]
    sent = []
    for k, to in enumerate(head_peers):
        sent.append(remote(logit, logit_got.at[k], lgs.at[k], lgr.at[k], {"head": to}))
        sent[-1].start()
    last()
    for gl in gls:
        gl.finish()
    for c in loads:
        c.wait()

    c2 = mla_scale * LOG2E
    group = LANES // half
    blocks = [slice(m, m + BLOCK) for m in range(0, key_count, BLOCK)]
    groups = heads // group
    kaug[:, :width] = lat_all[...]
    lane = lax.broadcasted_iota(jnp.int32, (key_count // 2, row_count), 1)
    for r in range(2):
        r0 = r * half
        ids = lax.broadcasted_iota(jnp.int32, (key_count, half), 0)
        kaug[:, width:] = jnp.where(ids < vis_ref[:, r0 : r0 + half], 0.0, neg_fill).astype(BF16)
        total[...] = jnp.zeros_like(total)

        def step(g, slot, factors, r0=r0):
            if g is not None:
                several = [latq[g * group + i][:, r0 : r0 + half] for i in range(group)]
                queries = jnp.concatenate([jnp.concatenate(several, axis=1), eye[...]], axis=0)
            peaks, sums = [], []
            for i, m in enumerate(blocks):
                if factors is not None:
                    t = ebuf[1 - slot, m, :] * factors[i]
                    total[m, :] += t[:, : LANES // 2] + t[:, LANES // 2 :]
                if g is not None:
                    s = jnp.dot(kaug[m, :], queries, preferred_element_type=F32)
                    peak = jnp.max(s, axis=0, keepdims=True)
                    e = jnp.exp2((s - peak) * c2)
                    ebuf[slot, m, :] = e
                    peaks.append(peak)
                    sums.append(jnp.sum(e, axis=0, keepdims=True))
            if g is None:
                return None
            highest = functools.reduce(jnp.maximum, peaks)
            scales = [jnp.exp2((peak - highest) * c2) for peak in peaks]
            inv = (1.0 / MLA_HEADS) / sum(f * x for f, x in zip(scales, sums))
            return tuple(f * inv for f in scales)

        factors = step(0, 0, None)

        def two(i, carry):
            return step(2 * i + 2, 0, step(2 * i + 1, 1, carry))

        factors = lax.fori_loop(0, groups // 2 - 1, two, factors)
        factors = step(groups - 1, 1, factors)
        step(None, 0, factors)

        t = total[...]
        t = t + pltpu.roll(t, half, 1)
        folded = jnp.where(lane < half, t[: key_count // 2], t[key_count // 2 :])
        fold[r] = folded
        part_out[r] = folded.astype(BF16)
        for k, to in enumerate(head_peers):
            sent.append(remote(part_out.at[r], part_got.at[k, r], ps.at[k, r], pr.at[k, r], {"head": to}))
            sent[-1].start()

    for k in range(nh - 1):
        remote(logit, logit_got.at[k], lgs.at[k], lgr.at[k], {"head": head_peers[k]}).wait_recv()
    both = logit[...]
    for k in range(nh - 1):
        both = both + logit_got[k]
    ids = lax.broadcasted_iota(jnp.int32, (key_count, row_count), 0)
    both = jnp.where(ids < vis_ref[...], both, neg_fill)
    weights = jnp.exp(both - jnp.max(both, axis=0, keepdims=True))
    total[...] = weights * (1.0 / jnp.sum(weights, axis=0, keepdims=True))
    folds = []
    for r in range(2):
        t = fold[r]
        for k in range(nh - 1):
            remote(part_out.at[r], part_got.at[k, r], ps.at[k, r], pr.at[k, r], {"head": head_peers[k]}).wait_recv()
            t = t + part_got[k, r].astype(F32)
        folds.append(t)
    upper = jnp.where(lane < half, folds[0], pltpu.roll(folds[1], half, 1))
    lower = jnp.where(lane < half, pltpu.roll(folds[0], half, 1), folds[1])
    slope[: key_count // 2, :] = (loss_weight * (total[: key_count // 2, :] - upper)).astype(BF16)
    slope[key_count // 2 :, :] = (loss_weight * (total[key_count // 2 :, :] - lower)).astype(BF16)

    owners = CHUNK // size
    columns = QUAD * row_count

    def term(o):
        rows = kg_out.at[pl.ds(pl.multiple_of(o * size, size), size), :]
        return remote(rows, got.at[me], ks.at[o], kr.at[me], {"seq": o})

    for i, m in enumerate(chunks):
        part = slope[m, :]
        tiled = jnp.concatenate([part] * QUAD, axis=1)
        acc = None
        for q in range(quads):
            edge = jnp.where(signs[q, m, :] > 0, tiled, 0).astype(BF16)
            signs[q, m, :] = edge
            t = jnp.dot(edge, wiq[q * columns : (q + 1) * columns, :], preferred_element_type=F32)
            acc = t if acc is None else acc + t
        acc = acc * dot_scale
        kg_all[m, :] = acc
        kg_out[m, :] = acc.astype(BF16)
        for o in range(i * owners, (i + 1) * owners):

            @pl.when(o < me)
            def _(o=o):
                term(o).start()

    def query_quad(q, _):
        base = pl.multiple_of(q * QUAD, QUAD)
        grad = jnp.dot(ikt[...], signs[q], preferred_element_type=F32)
        dots = jnp.sum(grad * iqt[q].astype(F32), axis=0, keepdims=True) * (dot_scale * head_scale)
        w = w_ref[pl.ds(base, QUAD), :] * (head_scale * dot_scale)
        for j in range(QUAD):
            cols = slice(j * row_count, (j + 1) * row_count)
            wgrad_ref[pl.ds(base + j, 1), :] = dots[:, cols]
            wide[pl.ds(base + j, row_count, stride=gheads), :] = (grad[:, cols] * w[j : j + 1]).T
        return 0

    lax.fori_loop(0, quads // 2, query_quad, 0)

    def collect(i, acc):
        remote(kg_out.at[pl.ds(0, size), :], got.at[i], ks.at[i], kr.at[i], {"seq": i}).wait_recv()
        return acc + got[i].astype(F32)

    mine[...] = lax.fori_loop(me + 1, n, collect, kg_all[pl.ds(pl.multiple_of(me * size, size), size), :])
    for k, to in enumerate(head_peers):
        sent.append(remote(mine, peer.at[k], hs.at[k], hr.at[k], {"head": to}))
        sent[-1].start()
    lax.fori_loop(quads // 2, quads, query_quad, 0)
    qgrad_ref[...] = wide[...].astype(BF16)
    acc = mine[...]
    for k in range(nh - 1):
        remote(mine, peer.at[k], hs.at[k], hr.at[k], {"head": head_peers[k]}).wait_recv()
        acc = acc + peer[k]
    kgrad_ref[...] = acc

    def settle(o, _):
        term(o).wait_send()
        return 0

    lax.fori_loop(0, me, settle, 0)
    gi.drain()
    for gl in gls:
        gl.drain()
    for copy in sent:
        copy.wait_send()


def body(n, nh, latent_queries, latent_keys, index_queries, index_keys, head_weights, visible):
    row_count, gheads, depth = index_queries.shape
    heads, width = latent_queries.shape[1:]
    size = latent_keys.shape[0]
    key_count = n * size
    half = row_count // 2
    quads = gheads // QUAD
    nz, ny = line_sizes(n)
    dma = pltpu.SemaphoreType.DMA
    parts = 8
    whole = pl.BlockSpec(memory_space=VMEM)
    hbm = pl.BlockSpec(memory_space=pltpu.HBM)
    hops = [dma((nz,)), dma((nz,)), dma((nz, ny)), dma((nz, ny)), dma((nz, ny)), dma((nz, ny))]
    query_grad, weight_grad, key_grad = pl.pallas_call(
        functools.partial(kernel, n, nh),
        out_shape=(
            VMEM((row_count * gheads, depth), BF16),
            VMEM((gheads, row_count), F32),
            VMEM((size, depth), F32),
        ),
        in_specs=[hbm, hbm, whole, whole, hbm, hbm],
        out_specs=(whole, whole, whole),
        scratch_shapes=[
            VMEM((heads, width, row_count), BF16),
            VMEM((row_count * gheads, depth), BF16),
            VMEM((row_count * gheads, depth), F32),
            VMEM((quads, depth, QUAD * row_count), BF16),
            VMEM((gheads * row_count, depth), BF16),
            VMEM((key_count, width), BF16),
            VMEM((key_count, depth), BF16),
            VMEM((depth, key_count), BF16),
            VMEM((key_count, width + half), BF16),
            VMEM((half, LANES), BF16),
            VMEM((key_count, row_count), F32),
            VMEM((2, key_count, LANES), F32),
            VMEM((quads, key_count, QUAD * row_count), BF16),
            VMEM((key_count, row_count), F32),
            VMEM((nh - 1, key_count, row_count), F32),
            VMEM((2, key_count // 2, row_count), BF16),
            VMEM((nh - 1, 2, key_count // 2, row_count), BF16),
            VMEM((key_count, row_count), BF16),
            VMEM((2, key_count // 2, row_count), F32),
            VMEM((key_count, depth), F32),
            VMEM((key_count, depth), BF16),
            VMEM((n, size, depth), BF16),
            VMEM((size, depth), F32),
            VMEM((nh - 1, size, depth), F32),
            dma((parts,)), dma, dma((1 + PIECES,)), *hops, *(hops * PIECES),
            dma((nh - 1,)), dma((nh - 1,)), dma((nh - 1, 2)), dma((nh - 1, 2)),
            dma((n,)), dma((n,)), dma((nh - 1,)), dma((nh - 1,)),
        ],
        compiler_params=pltpu.CompilerParams(
            collective_id=0, has_side_effects=True, vmem_limit_bytes=58 * 2**20
        ),
        name="indexer_warmup",
    )(
        latent_keys, index_keys, head_weights.T, visible.reshape(1, row_count),
        jnp.transpose(latent_queries, (1, 2, 0)), index_queries.reshape(row_count * gheads, depth),
    )
    return query_grad.reshape(row_count, gheads, depth), weight_grad.T, key_grad


def solution(mesh):
    placed = (
        P("seq", "head", None),
        P("seq", None),
        P("seq", "head", None),
        P("seq", None),
        P("seq", "head"),
        P("seq"),
    )
    return jax.shard_map(
        functools.partial(body, mesh.shape["seq"], mesh.shape["head"]),
        mesh=mesh,
        in_specs=placed,
        out_specs=(P("seq", "head", None), P("seq", "head"), P("seq", None)),
        check_vma=False,
    )
```

```python
import functools
import jax
import jax.numpy as jnp
from jax import lax
from jax.experimental import pallas as pl
from jax.experimental.pallas import tpu as pltpu
from jax.sharding import PartitionSpec as P

MLA_HEADS = 128
INDEX_HEADS = 64
LOG2E = 1.4426950408889634

mla_scale = 192.0 ** (-0.5)
loss_weight = 16.0
neg_fill = -1e30
MESH = pl.DeviceIdType.MESH
VMEM = pltpu.VMEM
BF16 = jnp.bfloat16
F32 = jnp.float32
LANES = 256
CHUNK = 256
QUAD = 4
PIECES = 2
BLOCK = 128


def line_sizes(n):
    ny = 2 if n <= 16 else 4
    return n // (2 * ny), ny


def remote(src, dst, ssem, rsem, device):
    return pltpu.make_async_remote_copy(
        src_ref=src, dst_ref=dst, send_sem=ssem, recv_sem=rsem, device_id=device, device_id_type=MESH
    )


class Gather:
    def __init__(self, n, ref, everything, lsem, zs, zr, ys, yr, cs, cr, piece=0, pieces=1):
        self.nz, self.ny = line_sizes(n)
        self.me = lax.axis_index("seq")
        self.core = self.me % 2
        self.y = (self.me // 2) % self.ny
        self.z = self.me // (2 * self.ny)
        self.full = ref.shape[0]
        self.size = self.full // pieces
        self.offset = piece * self.size
        self.ref, self.everything = ref.at[pl.ds(self.offset, self.size), :], everything
        self.lsem, self.zs, self.zr, self.ys, self.yr, self.cs, self.cr = lsem, zs, zr, ys, yr, cs, cr
        self.pending = []

    def at(self, zz, yy, cc):
        return (zz * self.ny + yy) * 2 + cc

    def rows(self, owner):
        start = pl.multiple_of(owner * self.full + self.offset, self.size)
        return self.everything.at[pl.ds(start, self.size), :]

    def send(self, owner, device, ssem, rsem):
        copy = remote(self.rows(owner), self.rows(owner), ssem, rsem, {"seq": device})
        copy.start()
        self.pending.append(copy)

    def receive(self, owner, ssem, rsem):
        other = {"seq": self.at(self.z, self.y, 1 - self.core)}
        remote(self.rows(owner), self.rows(owner), ssem, rsem, other).wait_recv()

    def keep(self):
        self.local = pltpu.make_async_copy(self.ref, self.rows(self.me), self.lsem)
        self.local.start()

    def start(self):
        z, y, core, nz, ny = self.z, self.y, self.core, self.nz, self.ny
        self.local.wait()
        for k in range(1, nz):
            self.send(self.me, self.at((z + k) % nz, y, core), self.zs.at[k], self.zr.at[k])
        for j in range(1, ny):
            self.send(self.me, self.at(z, (y + j) % ny, core), self.ys.at[0, j], self.yr.at[0, j])
        self.send(self.me, self.at(z, y, 1 - core), self.cs.at[0, 0], self.cr.at[0, 0])

    def pass_z(self, k):
        z, y, core, nz, ny = self.z, self.y, self.core, self.nz, self.ny
        owner = self.at((z - k + nz) % nz, y, core)
        self.receive(owner, self.zs.at[k], self.zr.at[k])
        for j in range(1, ny):
            self.send(owner, self.at(z, (y + j) % ny, core), self.ys.at[k, j], self.yr.at[k, j])
        self.send(owner, self.at(z, y, 1 - core), self.cs.at[k, 0], self.cr.at[k, 0])

    def pass_y(self, k):
        z, y, core, nz, ny = self.z, self.y, self.core, self.nz, self.ny
        for j in range(1, ny):
            owner = self.at((z - k + nz) % nz, (y - j + ny) % ny, core)
            self.receive(owner, self.ys.at[k, j], self.yr.at[k, j])
            self.send(owner, self.at(z, y, 1 - core), self.cs.at[k, j], self.cr.at[k, j])

    def finish(self):
        z, y, core, nz, ny = self.z, self.y, self.core, self.nz, self.ny
        for k in range(nz):
            for j in range(ny):
                owner = self.at((z - k + nz) % nz, (y - j + ny) % ny, 1 - core)
                self.receive(owner, self.cs.at[k, j], self.cr.at[k, j])

    def drain(self):
        for copy in self.pending:
            copy.wait_send()
        self.pending = []


def kernel(
    n, nh, lat_ref, idx_ref, w_ref, vis_ref, latq_hbm, iq_hbm,
    qgrad_ref, wgrad_ref, kgrad_ref,
    latq, iqraw, wide, iqt, wiq, lat_all, idx_all, ikt, kaug, eye, total, ebuf, signs,
    logit, logit_got, part_out, part_got, slope, fold, kg_all, kg_out, got, mine, peer,
    qsem, isem, glsem, zs0, zr0, ys0, yr0, cs0, cr0, *hops,
):
    lgs, lgr, ps, pr, ks, kr, hs, hr = hops[6 * PIECES :]
    me = lax.axis_index("seq")
    head = lax.axis_index("head")
    heads, width, row_count = latq.shape
    key_count = lat_all.shape[0]
    depth = idx_ref.shape[1]
    gheads = w_ref.shape[0]
    size = idx_ref.shape[0]
    half = row_count // 2
    dot_scale = float(depth) ** (-0.5)
    head_scale = INDEX_HEADS ** (-0.5)
    nz, ny = line_sizes(n)

    barrier = pltpu.get_barrier_semaphore()
    for k in range(1, n):
        pl.semaphore_signal(barrier, inc=1, device_id={"seq": (me + k) % n}, device_id_type=MESH)
    for k in range(1, nh):
        pl.semaphore_signal(barrier, inc=1, device_id={"head": (head + k) % nh}, device_id_type=MESH)
    gi = Gather(n, idx_ref, idx_all, glsem.at[0], zs0, zr0, ys0, yr0, cs0, cr0)
    gls = [
        Gather(n, lat_ref, lat_all, glsem.at[1 + i], *hops[6 * i : 6 * i + 6], piece=i, pieces=PIECES)
        for i in range(PIECES)
    ]
    gi.keep()
    for gl in gls:
        gl.keep()
    load_iq = pltpu.make_async_copy(iq_hbm, iqraw, isem)
    load_iq.start()
    parts = qsem.shape[0]
    per = heads // parts
    loads = [
        pltpu.make_async_copy(latq_hbm.at[pl.ds(i * per, per)], latq.at[pl.ds(i * per, per)], qsem.at[i])
        for i in range(parts)
    ]
    for c in loads:
        c.start()
    pl.semaphore_wait(barrier, n - 1 + nh - 1)
    gi.start()
    gls[0].start()

    load_iq.wait()
    wide[...] = iqraw[...].astype(F32)
    wcol = (w_ref[...] * head_scale).T

    for g in range(gheads):
        a = wide[pl.ds(g, row_count, stride=gheads), :]
        iqt[g // QUAD, :, (g % QUAD) * row_count : (g % QUAD + 1) * row_count] = a.T.astype(BF16)
        wiq[pl.ds(g * row_count, row_count), :] = (a * wcol[:, g : g + 1]).astype(BF16)

    def hide(r0):
        ids = lax.broadcasted_iota(jnp.int32, (key_count, half), 0)
        kaug[:, width:] = jnp.where(ids < vis_ref[:, r0 : r0 + half], 0.0, neg_fill).astype(BF16)

    hide(0)
    total[...] = jnp.zeros_like(total)
    first = lax.broadcasted_iota(jnp.int32, (half, LANES), 0)
    second = lax.broadcasted_iota(jnp.int32, (half, LANES), 1)
    eye[...] = jnp.where(first == second % half, 1.0, 0.0).astype(BF16)

    for k in range(1, nz):
        gi.pass_z(k)
    gls[0].drain()
    gls[1].start()
    for k in range(nz):
        gi.pass_y(k)
    for k in range(1, nz):
        gls[0].pass_z(k)
    gi.finish()
    ikt[...] = idx_all[...].astype(F32).T.astype(BF16)
    logit[...] = jnp.zeros_like(logit)

    chunks = [slice(m, m + CHUNK) for m in range(0, key_count, CHUNK)]
    quads = gheads // QUAD

    def index_quad(q, _):
        w = w_ref[pl.ds(pl.multiple_of(q * QUAD, QUAD), QUAD), :] * (head_scale * dot_scale)
        queries = iqt[q]
        for m in chunks:
            p = jnp.dot(idx_all[m, :], queries, preferred_element_type=F32)
            signs[q, m, :] = p.astype(BF16)
            added = None
            for j in range(QUAD):
                x = jnp.maximum(p[:, j * row_count : (j + 1) * row_count], 0.0) * w[j : j + 1]
                added = x if added is None else added + x
            logit[m, :] += added
        return 0

    events = []
    for gl in gls[1:]:
        events += [functools.partial(gl.pass_z, k) for k in range(1, nz)]
    for gl in gls:
        events += [functools.partial(gl.pass_y, k) for k in range(nz)]
    last = events.pop()
    done = 0
    for event in events:
        event()
        if done < quads:
            index_quad(done, 0)
            done += 1
    lax.fori_loop(done, quads, index_quad, 0)
    head_peers = [(head + k) % nh for k in range(1, nh)]
    sent = []
    for k, to in enumerate(head_peers):
        sent.append(remote(logit, logit_got.at[k], lgs.at[k], lgr.at[k], {"head": to}))
        sent[-1].start()
    last()
    for gl in gls:
        gl.finish()
    for c in loads:
        c.wait()

    c2 = mla_scale * LOG2E
    group = LANES // half
    blocks = [slice(m, m + BLOCK) for m in range(0, key_count, BLOCK)]
    groups = heads // group
    kaug[:, :width] = lat_all[...]
    lane = lax.broadcasted_iota(jnp.int32, (key_count // 2, row_count), 1)
    for r in range(2):
        r0 = r * half
        if r > 0:
            hide(r0)
            total[...] = jnp.zeros_like(total)

        def step(g, slot, factors, r0=r0):
            if g is not None:
                several = [latq[g * group + i][:, r0 : r0 + half] for i in range(group)]
                queries = jnp.concatenate([jnp.concatenate(several, axis=1), eye[...]], axis=0)
            peaks, sums = [], []
            for i, m in enumerate(blocks):
                if factors is not None:
                    t = ebuf[1 - slot, m, :] * factors[i]
                    total[m, :] += t[:, : LANES // 2] + t[:, LANES // 2 :]
                if g is not None:
                    s = jnp.dot(kaug[m, :], queries, preferred_element_type=F32)
                    peak = jnp.max(s, axis=0, keepdims=True)
                    e = jnp.exp2((s - peak) * c2)
                    ebuf[slot, m, :] = e
                    peaks.append(peak)
                    sums.append(jnp.sum(e, axis=0, keepdims=True))
            if g is None:
                return None
            highest = functools.reduce(jnp.maximum, peaks)
            scales = [jnp.exp2((peak - highest) * c2) for peak in peaks]
            inv = (1.0 / MLA_HEADS) / sum(f * x for f, x in zip(scales, sums))
            return tuple(f * inv for f in scales)

        factors = step(0, 0, None)

        def two(i, carry):
            return step(2 * i + 2, 0, step(2 * i + 1, 1, carry))

        factors = lax.fori_loop(0, groups // 2 - 1, two, factors)
        factors = step(groups - 1, 1, factors)
        step(None, 0, factors)

        t = total[...]
        t = t + pltpu.roll(t, half, 1)
        folded = jnp.where(lane < half, t[: key_count // 2], t[key_count // 2 :])
        fold[r] = folded
        part_out[r] = folded.astype(BF16)
        for k, to in enumerate(head_peers):
            sent.append(remote(part_out.at[r], part_got.at[k, r], ps.at[k, r], pr.at[k, r], {"head": to}))
            sent[-1].start()

    for k in range(nh - 1):
        remote(logit, logit_got.at[k], lgs.at[k], lgr.at[k], {"head": head_peers[k]}).wait_recv()
    both = logit[...]
    for k in range(nh - 1):
        both = both + logit_got[k]
    ids = lax.broadcasted_iota(jnp.int32, (key_count, row_count), 0)
    both = jnp.where(ids < vis_ref[...], both, neg_fill)
    weights = jnp.exp(both - jnp.max(both, axis=0, keepdims=True))
    total[...] = weights * (1.0 / jnp.sum(weights, axis=0, keepdims=True))
    folds = []
    for r in range(2):
        t = fold[r]
        for k in range(nh - 1):
            remote(part_out.at[r], part_got.at[k, r], ps.at[k, r], pr.at[k, r], {"head": head_peers[k]}).wait_recv()
            t = t + part_got[k, r].astype(F32)
        folds.append(t)
    upper = jnp.where(lane < half, folds[0], pltpu.roll(folds[1], half, 1))
    lower = jnp.where(lane < half, pltpu.roll(folds[0], half, 1), folds[1])
    slope[: key_count // 2, :] = (loss_weight * (total[: key_count // 2, :] - upper)).astype(BF16)
    slope[key_count // 2 :, :] = (loss_weight * (total[key_count // 2 :, :] - lower)).astype(BF16)

    owners = CHUNK // size
    columns = QUAD * row_count

    def term(o):
        rows = kg_out.at[pl.ds(pl.multiple_of(o * size, size), size), :]
        return remote(rows, got.at[me], ks.at[o], kr.at[me], {"seq": o})

    for i, m in enumerate(chunks):
        part = slope[m, :]
        tiled = jnp.concatenate([part] * QUAD, axis=1)
        acc = None
        for q in range(quads):
            edge = jnp.where(signs[q, m, :] > 0, tiled, 0).astype(BF16)
            signs[q, m, :] = edge
            t = jnp.dot(edge, wiq[q * columns : (q + 1) * columns, :], preferred_element_type=F32)
            acc = t if acc is None else acc + t
        acc = acc * dot_scale
        kg_all[m, :] = acc
        kg_out[m, :] = acc.astype(BF16)
        for o in range(i * owners, (i + 1) * owners):

            @pl.when(o < me)
            def _(o=o):
                term(o).start()

    def query_quad(q, _):
        base = pl.multiple_of(q * QUAD, QUAD)
        grad = jnp.dot(ikt[...], signs[q], preferred_element_type=F32)
        dots = jnp.sum(grad * iqt[q].astype(F32), axis=0, keepdims=True) * (dot_scale * head_scale)
        w = w_ref[pl.ds(base, QUAD), :] * (head_scale * dot_scale)
        for j in range(QUAD):
            cols = slice(j * row_count, (j + 1) * row_count)
            wgrad_ref[pl.ds(base + j, 1), :] = dots[:, cols]
            wide[pl.ds(base + j, row_count, stride=gheads), :] = (grad[:, cols] * w[j : j + 1]).T
        return 0

    lax.fori_loop(0, quads // 2, query_quad, 0)

    def collect(i, acc):
        remote(kg_out.at[pl.ds(0, size), :], got.at[i], ks.at[i], kr.at[i], {"seq": i}).wait_recv()
        return acc + got[i].astype(F32)

    mine[...] = lax.fori_loop(me + 1, n, collect, kg_all[pl.ds(pl.multiple_of(me * size, size), size), :])
    for k, to in enumerate(head_peers):
        sent.append(remote(mine, peer.at[k], hs.at[k], hr.at[k], {"head": to}))
        sent[-1].start()
    lax.fori_loop(quads // 2, quads, query_quad, 0)
    qgrad_ref[...] = wide[...].astype(BF16)
    acc = mine[...]
    for k in range(nh - 1):
        remote(mine, peer.at[k], hs.at[k], hr.at[k], {"head": head_peers[k]}).wait_recv()
        acc = acc + peer[k]
    kgrad_ref[...] = acc

    def settle(o, _):
        term(o).wait_send()
        return 0

    lax.fori_loop(0, me, settle, 0)
    gi.drain()
    for gl in gls:
        gl.drain()
    for copy in sent:
        copy.wait_send()


def body(n, nh, latent_queries, latent_keys, index_queries, index_keys, head_weights, visible):
    row_count, gheads, depth = index_queries.shape
    heads, width = latent_queries.shape[1:]
    size = latent_keys.shape[0]
    key_count = n * size
    half = row_count // 2
    quads = gheads // QUAD
    nz, ny = line_sizes(n)
    dma = pltpu.SemaphoreType.DMA
    parts = 8
    whole = pl.BlockSpec(memory_space=VMEM)
    hbm = pl.BlockSpec(memory_space=pltpu.HBM)
    hops = [dma((nz,)), dma((nz,)), dma((nz, ny)), dma((nz, ny)), dma((nz, ny)), dma((nz, ny))]
    query_grad, weight_grad, key_grad = pl.pallas_call(
        functools.partial(kernel, n, nh),
        out_shape=(
            VMEM((row_count * gheads, depth), BF16),
            VMEM((gheads, row_count), F32),
            VMEM((size, depth), F32),
        ),
        in_specs=[hbm, hbm, whole, whole, hbm, hbm],
        out_specs=(whole, whole, whole),
        scratch_shapes=[
            VMEM((heads, width, row_count), BF16),
            VMEM((row_count * gheads, depth), BF16),
            VMEM((row_count * gheads, depth), F32),
            VMEM((quads, depth, QUAD * row_count), BF16),
            VMEM((gheads * row_count, depth), BF16),
            VMEM((key_count, width), BF16),
            VMEM((key_count, depth), BF16),
            VMEM((depth, key_count), BF16),
            VMEM((key_count, width + half), BF16),
            VMEM((half, LANES), BF16),
            VMEM((key_count, row_count), F32),
            VMEM((2, key_count, LANES), F32),
            VMEM((quads, key_count, QUAD * row_count), BF16),
            VMEM((key_count, row_count), F32),
            VMEM((nh - 1, key_count, row_count), F32),
            VMEM((2, key_count // 2, row_count), BF16),
            VMEM((nh - 1, 2, key_count // 2, row_count), BF16),
            VMEM((key_count, row_count), BF16),
            VMEM((2, key_count // 2, row_count), F32),
            VMEM((key_count, depth), F32),
            VMEM((key_count, depth), BF16),
            VMEM((n, size, depth), BF16),
            VMEM((size, depth), F32),
            VMEM((nh - 1, size, depth), F32),
            dma((parts,)), dma, dma((1 + PIECES,)), *hops, *(hops * PIECES),
            dma((nh - 1,)), dma((nh - 1,)), dma((nh - 1, 2)), dma((nh - 1, 2)),
            dma((n,)), dma((n,)), dma((nh - 1,)), dma((nh - 1,)),
        ],
        compiler_params=pltpu.CompilerParams(
            collective_id=0, has_side_effects=True, vmem_limit_bytes=58 * 2**20
        ),
        name="indexer_warmup",
    )(
        latent_keys, index_keys, head_weights.T, visible.reshape(1, row_count),
        jnp.transpose(latent_queries, (1, 2, 0)), index_queries.reshape(row_count * gheads, depth),
    )
    return query_grad.reshape(row_count, gheads, depth), weight_grad.T, key_grad


def solution(mesh):
    placed = (
        P("seq", "head", None),
        P("seq", None),
        P("seq", "head", None),
        P("seq", None),
        P("seq", "head"),
        P("seq"),
    )
    return jax.shard_map(
        functools.partial(body, mesh.shape["seq"], mesh.shape["head"]),
        mesh=mesh,
        in_specs=placed,
        out_specs=(P("seq", "head", None), P("seq", "head"), P("seq", None)),
        check_vma=False,
    )
```
